32 devices in a mesh: gx: 16 (over z, x, core), gy: 2 (over y).
Axes of the slice: x: 2, y: 2, z: 4, core: 2. Of those that a mesh axis runs over, the one named last changes fastest.
Arguments:
- density: float32 [32, 24, 6912], P('gx', None, 'gy'), may hold values from 0.05 to 1
- gains_a: float32 [8, 24, 24, 24], replicated, may hold values from -6 to 6
- gains_b: float32 [8, 24, 24, 24], replicated, may hold values from -6 to 6
- loss_rates: float32 [24, 24, 24], replicated, may hold values from 0.1 to 1
Outputs:
- evolved: float32 [32, 24, 6912], P('gx', None, 'gy')
The draws below stay inside these ranges and needn't reach their ends.
All inputs are finite; a program needn't handle non-finite values.
Results may differ from the reference program's by a relative error of at most 0.0001.
Values sent between devices are 32-bit elements; how exact they have to be, the bound alone decides.
No kernel may reach another device: no remote copies, remote signals or barrier semaphores. Data moves between devices by JAX's collectives and lax.ppermute only.
A program may use at most 128 MiB of HBM per device.

```python
import math
import jax
import jax.numpy as jnp
from jax import lax

V = 24
P_SIZE = 8
NX = 32
NY = 12


def level_of(own_key, dims, split, least, top_value):
    def one(axis_at, parts):
        draws = jax.random.uniform(jax.random.fold_in(jax.random.fold_in(own_key, 6), axis_at), (parts,), jnp.float32, least / len(split), top_value / len(split))
        return jnp.repeat(jnp.exp(draws), dims[axis_at] // parts).reshape((-1,) + (1,) * (len(dims) - axis_at - 1))

    loudness = one(*split[0])
    for cut in split[1:]:
        loudness = loudness * one(*cut)
    return loudness


def scatter_about(rng, dims, spread, most, held_as=jnp.bfloat16):
    return jnp.clip(spread * jax.random.normal(rng, dims, jnp.float32), -most, most).astype(held_as)


def setup_inputs(seed: int = 0) -> dict:
    splits = jax.random.split(jax.random.key(seed), 5)
    return {
        "density": jnp.clip(jnp.exp(math.log(1.0) - 2.9957323 * jax.random.uniform(splits[0], (NX, V, NY * V * V), jnp.float32) ** level_of(splits[0], (NX, V, NY * V * V), ((0, 16), (2, 2)), -0.2, 0.2)), 0.05, 1.0),
        "gains_a": scatter_about(splits[1], (P_SIZE, V, V, V), 1.0, 6.0, jnp.float32),
        "gains_b": scatter_about(splits[2], (P_SIZE, V, V, V), 1.0, 6.0, jnp.float32),
        "loss_rates": jnp.clip(jnp.exp(jax.random.uniform(splits[3], (V, V, V), jnp.float32, math.log(0.1), math.log(1.0))), 0.1, 1.0),
    }


highest = lax.Precision.HIGHEST
courant_max = 1.6
collide_step = 0.2

def cosine_table(count):
    freq = jnp.arange(count, dtype=jnp.float32)[:, None]
    points = jnp.arange(count, dtype=jnp.float32)[None, :]
    scale = jnp.where(freq == 0, jnp.sqrt(1.0 / count), jnp.sqrt(2.0 / count))
    return scale * jnp.cos(jnp.pi * (2.0 * points + 1.0) * freq / (2.0 * count))

def courant(count):
    speeds = jnp.arange(count, dtype=jnp.float32) - (count - 1) / 2.0
    return courant_max * jnp.abs(speeds) / ((count - 1) / 2.0)

def weights(numbers):
    return (1.0 - 1.5 * numbers + 0.5 * numbers * numbers, 2.0 * numbers - numbers * numbers, 0.5 * (numbers * numbers - numbers))

def transform(table, field):
    field = jnp.einsum('ka,xaybc->xkybc', table, field, precision=highest)
    field = jnp.einsum('kb,xaybc->xaykc', table, field, precision=highest)
    return jnp.einsum('kc,xaybc->xaybk', table, field, precision=highest)

def collide(field, cosine, gains_a, gains_b, loss_rates):
    spectrum = transform(cosine, field)
    loss = field * transform(cosine.T, loss_rates[:, None, :, :] * spectrum)
    gain = jnp.zeros_like(field)
    for term in range(gains_a.shape[0]):
        first = transform(cosine.T, gains_a[term][:, None, :, :] * spectrum)
        second = transform(cosine.T, gains_b[term][:, None, :, :] * spectrum)
        gain = gain + first * second
    return field + collide_step * (gain - loss)

def reference(density, gains_a, gains_b, loss_rates):
    middle = V // 2
    numbers = courant(V)
    cosine = cosine_table(V)
    field = density.reshape(NX, V, NY, V, V)
    pw0, pw1, pw2 = weights(numbers[middle:][None, :, None, None, None])
    nw0, nw1, nw2 = weights(numbers[:middle][None, :, None, None, None])
    positive = field[:, middle:]
    negative = field[:, :middle]
    pos_new = pw0 * positive + pw1 * jnp.roll(positive, 1, 0) + pw2 * jnp.roll(positive, 2, 0)
    neg_new = nw0 * negative + nw1 * jnp.roll(negative, -1, 0) + nw2 * jnp.roll(negative, -2, 0)
    field = jnp.concatenate([neg_new, pos_new], 1)
    field = collide(field, cosine, gains_a, gains_b, loss_rates)
    pw0, pw1, pw2 = weights(numbers[middle:][None, None, None, :, None])
    nw0, nw1, nw2 = weights(numbers[:middle][None, None, None, :, None])
    positive = field[:, :, :, middle:]
    negative = field[:, :, :, :middle]
    pos_new = pw0 * positive + pw1 * jnp.roll(positive, 1, 2) + pw2 * jnp.roll(positive, 2, 2)
    neg_new = nw0 * negative + nw1 * jnp.roll(negative, -1, 2) + nw2 * jnp.roll(negative, -2, 2)
    field = jnp.concatenate([neg_new, pos_new], 3)
    field = collide(field, cosine, gains_a, gains_b, loss_rates)
    return field.reshape(NX, V, NY * V * V)
```

```python
import functools

import jax
import jax.numpy as jnp
import numpy as np
from jax import lax
from jax.experimental import pallas as pl
from jax.experimental.pallas import tpu as pltpu
from jax.sharding import PartitionSpec as P

courant_max = 1.6
collide_step = 0.2
lanes = 128
bf16 = jnp.bfloat16
f32 = jnp.float32
dot = functools.partial(jnp.dot, preferred_element_type=f32)


def passed_along(value, axis, steps):
    count = lax.axis_size(axis)
    pairs = [(source, (source + steps) % count) for source in range(count)]
    return lax.ppermute(value, axis, pairs)


def cosine_table(count):
    freq = np.arange(count)[:, None]
    points = np.arange(count)[None, :]
    scale = np.where(freq == 0, np.sqrt(1.0 / count), np.sqrt(2.0 / count))
    return scale * np.cos(np.pi * (2.0 * points + 1.0) * freq / (2.0 * count))


def two_parts(table):
    high = np.asarray(table, np.float32).astype(bf16)
    return high, (table - high.astype(np.float64)).astype(np.float32).astype(bf16)


def courant_weights(count):
    speeds = np.arange(count) - (count - 1) / 2.0
    a = courant_max * np.abs(speeds) / ((count - 1) / 2.0)
    return np.stack([1.0 - 1.5 * a + 0.5 * a * a, 2.0 * a - a * a, 0.5 * (a * a - a)])


def sign(s, q):
    return -1.0 if ((s >> 1) & (q >> 1)) ^ (s & 1 & q) else 1.0


def block_table(count, q):
    c = cosine_table(count)
    half = count // 2
    return np.kron(c[q >> 1 :: 2, :half], c[q & 1 :: 2, :half])


def point_lanes(count):
    half = count // 2
    block = half * half
    rest = block - lanes
    source = np.full(5 * lanes, -1, np.int32)
    for s in range(4):
        for m in range(block):
            j, l = divmod(m, half)
            y = count - 1 - j if s >> 1 else j
            z = count - 1 - l if s & 1 else l
            if m < lanes:
                source[s * lanes + m] = y * count + z
            else:
                for copy in range(2):
                    source[4 * lanes + copy * 4 * rest + s * rest + m - lanes] = y * count + z
    return source


def mode_lanes(count):
    half = count // 2
    block = half * half
    rest = block - lanes
    source = np.full(6 * lanes, -1, np.int32)
    for q in range(4):
        for m in range(block):
            j, l = divmod(m, half)
            place = (2 * j + (q >> 1)) * count + 2 * l + (q & 1)
            if m < lanes:
                source[q * lanes + m] = place
            else:
                for copy in range(3):
                    source[(4 + q // 2) * lanes + copy * 2 * rest + (q % 2) * rest + m - lanes] = place
    return source


def inverse_tables(count):
    rest = (count // 2) ** 2 - lanes
    out = np.zeros((4, 4 * lanes, 2 * lanes), bf16)
    for q in range(4):
        table = block_table(count, q)
        wide = np.zeros((table.shape[0], 2 * lanes))
        wide[:, :lanes] = table[:, :lanes]
        for s in range(4):
            for copy in range(2):
                at = lanes + copy * 4 * rest + s * rest
                wide[:, at : at + rest] = sign(s, q) * table[:, lanes:]
        high, low = two_parts(wide)
        out[q, :lanes] = high[:lanes]
        out[q, lanes : 2 * lanes] = high[:lanes]
        out[q, 2 * lanes : 3 * lanes] = low[:lanes]
        for copy, part in enumerate((high, high, low)):
            at = 3 * lanes + copy * 2 * rest + (q % 2) * rest
            out[q, at : at + rest] = part[lanes:]
    return out


def forward_tables(count):
    rest = (count // 2) ** 2 - lanes
    out = np.zeros((4, 5 * lanes, 2 * lanes), bf16)
    for q in range(4):
        table = block_table(count, q).T
        wide = np.zeros((table.shape[0], 2 * lanes))
        wide[:, :lanes] = table[:, :lanes]
        for copy in range(3):
            at = lanes + copy * 2 * rest + (q % 2) * rest
            wide[:, at : at + rest] = table[:, lanes:]
        high, low = two_parts(wide)
        out[q, :lanes] = high[:lanes]
        out[q, lanes : 2 * lanes] = high[:lanes]
        out[q, 2 * lanes : 3 * lanes] = low[:lanes]
        for s in range(4):
            for at, part in ((3 * lanes, high), (3 * lanes + 4 * rest, high), (4 * lanes, low)):
                at = at + s * rest
                out[q, at : at + rest] = (sign(s, q) * part[lanes:].astype(np.float32)).astype(bf16)
    return out


def row_tables(count, cells):
    c = cosine_table(count)
    result = []
    for table in (c, c.T):
        high, low = two_parts(np.kron(np.eye(cells), table))
        result.append(np.concatenate([high, high, low], axis=1))
    return np.stack(result)


def split(value):
    high = value.astype(bf16)
    return high, (value - high.astype(f32)).astype(bf16)


def lane_index():
    return lax.broadcasted_iota(jnp.int32, (1, lanes), 1)


def tile(value, at):
    return value[:, at * lanes : (at + 1) * lanes]


def crossed(v0, v1, v2, v3):
    t0, t1, t2, t3 = v0 + v1, v0 - v1, v2 + v3, v2 - v3
    return t0 + t2, t1 + t3, t0 - t2, t1 - t3


def stacked_rows(value):
    high, low = split(value)
    return jnp.concatenate([high, low, high], axis=0)


def forward(value, table_ref, row_table, rest):
    mixed = crossed(*[tile(value, s) for s in range(4)])
    high, low = split(tile(value, 4))
    both = jnp.where(lane_index() < 4 * rest, high.astype(f32), low.astype(f32)).astype(bf16)
    found = []
    for q in range(4):
        q_high, q_low = split(mixed[q])
        found.append(dot(jnp.concatenate([q_high, q_low, q_high, both, high], axis=1), table_ref[q]))
    modes = jnp.concatenate(
        [tile(v, 0) for v in found] + [tile(found[0], 1) + tile(found[1], 1), tile(found[2], 1) + tile(found[3], 1)],
        axis=1,
    )
    return dot(row_table, stacked_rows(modes))


def inverse_plane(modes, table_ref, rest):
    low_lanes = (lane_index() >= 2 * rest) & (lane_index() < 4 * rest)
    both = []
    for pair in range(2):
        value = tile(modes, 4 + pair)
        high = value.astype(bf16).astype(f32)
        both.append(jnp.where(low_lanes, value - high, high).astype(bf16))
    found = []
    for q in range(4):
        high, low = split(tile(modes, q))
        found.append(dot(jnp.concatenate([high, low, high, both[q // 2]], axis=1), table_ref[q]))
    main = crossed(*[tile(v, 0) for v in found])
    last = (tile(found[0], 1) + tile(found[1], 1)) + (tile(found[2], 1) + tile(found[3], 1))
    return jnp.concatenate(list(main) + [last], axis=1)


def collide(field_ref, modes_ref, sum_ref, kernel_ref, inverse_ref, forward_ref, rows_ref, count, rest, terms):
    units, rows, _ = field_ref.shape
    cells = rows // count
    fwd_rows = rows_ref[0]
    inv_rows = rows_ref[1]

    def scaled(u, factor):
        modes = modes_ref[u].reshape(cells, count, 6 * lanes)
        return (modes * factor[None]).reshape(rows, 6 * lanes)

    for u in range(units):
        modes_ref[u] = forward(field_ref[u], forward_ref, fwd_rows, rest)
    for u in range(units):
        plane = inverse_plane(scaled(u, kernel_ref[2 * terms]), inverse_ref, rest)
        sum_ref[u] = -field_ref[u] * dot(inv_rows, stacked_rows(plane))

    def term(p, carry):
        for u in range(units):
            both = jnp.concatenate([scaled(u, kernel_ref[p]), scaled(u, kernel_ref[terms + p])], axis=0)
            plane = inverse_plane(both, inverse_ref, rest)
            pair = jnp.concatenate([stacked_rows(plane[:rows]), stacked_rows(plane[rows:])], axis=1)
            found = dot(inv_rows, pair)
            sum_ref[u] += found[:, : 5 * lanes] * found[:, 5 * lanes :]
        return carry

    lax.fori_loop(0, terms, term, 0)
    for u in range(units):
        field_ref[u] = field_ref[u] + collide_step * sum_ref[u]


def one_hot(source_row, rows):
    index = lax.broadcasted_iota(jnp.int32, (rows, source_row.shape[1]), 0)
    return jnp.where(index == source_row, 1.0, 0.0).astype(bf16)


def moved(value, table):
    high, low = split(value)
    return dot(high, table) + dot(low, table)


def pack_kernel(count, source_ref, a_ref, b_ref, loss_ref, out_ref):
    table = one_hot(source_ref[...], count * count)

    def packed(ref, start, matrices):
        rows = matrices * count
        parts = [ref[pl.ds(start * count * count + k, rows, stride=count), :] for k in range(count)]
        return moved(jnp.concatenate(parts, axis=1), table).reshape(matrices, count, 6 * lanes)

    terms = a_ref.shape[0] // (count * count)
    out_ref[:terms] = packed(a_ref, 0, terms)
    out_ref[terms : 2 * terms] = packed(b_ref, 0, terms)
    out_ref[2 * terms :] = packed(loss_ref, 0, 1)


def cell_order(cells_y):
    return list(range(0, cells_y, 2)) + list(range(1, cells_y, 2))


def first_kernel(
    count, rest, terms, cells_y,
    density_ref, below_ref, above_ref, kernel_ref, inverse_ref, forward_ref, rows_ref, speed_ref, source_ref,
    field_ref, up_ref, down_ref, modes_ref, sum_ref, rim_ref,
):
    cells_x = density_ref.shape[0]
    middle = count // 2
    plane = count * count
    for i in range(2):
        rim_ref[i, :middle] = above_ref[i]
        rim_ref[i, middle:] = below_ref[i]
    positive = lax.broadcasted_iota(jnp.int32, (count, 1), 0) >= middle
    tables = [one_hot(source_ref[k : k + 1], 5 * lanes) for k in range(2)]

    def behind(x):
        return density_ref[x] if x >= 0 else rim_ref[x + 2]

    def ahead(x):
        return density_ref[x] if x < cells_x else rim_ref[x - cells_x]

    for x in range(cells_x):
        w0, w1, w2 = [speed_ref[:, k : k + 1] for k in range(3)]
        near = jnp.where(positive, behind(x - 1), ahead(x + 1))
        far = jnp.where(positive, behind(x - 2), ahead(x + 2))
        moved_on = w0 * density_ref[x] + w1 * near + w2 * far
        pieces = []
        for odd in range(2):
            parts = []
            for y in range(odd, cells_y, 2):
                at = y * plane - odd * (lanes // 2)
                parts.append(moved_on[:, at : at + 5 * lanes])
            pieces.append(moved(jnp.concatenate(parts, axis=0), tables[odd]))
        field_ref[x] = jnp.concatenate(pieces, axis=0)
    collide(field_ref, modes_ref, sum_ref, kernel_ref, inverse_ref, forward_ref, rows_ref, count, rest, terms)
    order = cell_order(cells_y)
    for x in range(cells_x):
        for k in range(2):
            at = order.index(cells_y - 2 + k) * count
            up_ref[x, k] = field_ref[x, at : at + count, 2 * lanes :]
            at = order.index(k) * count
            down_ref[x, k, :, : 2 * lanes] = field_ref[x, at : at + count, : 2 * lanes]
            down_ref[x, k, :, 2 * lanes :] = field_ref[x, at : at + count, 4 * lanes :]


def second_kernel(
    count, rest, terms, cells_y,
    given_ref, below_ref, above_ref, kernel_ref, inverse_ref, forward_ref, rows_ref, speed_ref, source_ref,
    out_ref, field_ref, modes_ref, sum_ref,
):
    cells_x = given_ref.shape[0]
    plane = count * count
    order = cell_order(cells_y)
    backward_last = (lane_index() // (2 * rest)) % 2 == 1
    for x in range(cells_x):

        def cell(y, part):
            if y < 0:
                return below_ref[x, y + 2, :, (part - 2) * lanes : (part - 1) * lanes]
            if y >= cells_y:
                at = part if part < 2 else 2
                return above_ref[x, y - cells_y, :, at * lanes : (at + 1) * lanes]
            at = order.index(y) * count
            return given_ref[x, at : at + count, part * lanes : (part + 1) * lanes]

        for y in range(cells_y):
            at = order.index(y) * count
            for part in range(5):
                w0, w1, w2 = [speed_ref[k : k + 1, part * lanes : (part + 1) * lanes] for k in range(3)]
                if part < 2:
                    near, far = cell(y + 1, part), cell(y + 2, part)
                elif part < 4:
                    near, far = cell(y - 1, part), cell(y - 2, part)
                else:
                    near = jnp.where(backward_last, cell(y - 1, part), cell(y + 1, part))
                    far = jnp.where(backward_last, cell(y - 2, part), cell(y + 2, part))
                field_ref[x, at : at + count, part * lanes : (part + 1) * lanes] = (
                    w0 * cell(y, part) + w1 * near + w2 * far
                )
    collide(field_ref, modes_ref, sum_ref, kernel_ref, inverse_ref, forward_ref, rows_ref, count, rest, terms)
    tables = [one_hot(source_ref[k : k + 1], 5 * lanes) for k in range(2)]
    half = (cells_y // 2) * count
    for x in range(cells_x):
        even = moved(field_ref[x, :half], tables[0])
        odd = moved(field_ref[x, half:], tables[1])
        for k in range(cells_y // 2):
            first = even[k * count : (k + 1) * count]
            second = odd[k * count : (k + 1) * count]
            pair = [tile(first, t) for t in range(4)] + [tile(first, 4) + tile(second, 0)]
            pair += [tile(second, t) for t in range(1, 5)]
            out_ref[x, :, 2 * k * plane : 2 * (k + 1) * plane] = jnp.concatenate(pair, axis=1)


def body(density, gains_a, gains_b, loss_rates):
    cells_x, count, _ = density.shape
    terms = gains_a.shape[0]
    middle = count // 2
    plane = count * count
    cells_y = density.shape[2] // plane
    rest = middle * middle - lanes
    rows = cells_y * count
    points = point_lanes(count)
    natural = np.full((2, 5 * lanes), -1, np.int32)
    for lane in range(4 * lanes + 4 * rest):
        natural[0, points[lane]] = lane
        natural[1, points[lane] + lanes // 2] = lane
    fold = np.where(points >= 0, np.stack([points, points + lanes // 2]), -1).astype(np.int32)
    weights = courant_weights(count)
    lane_speed = np.where(points >= 0, weights[:, points // count], 0.0).astype(np.float32)
    inverse = jnp.asarray(inverse_tables(count))
    forward_table = jnp.asarray(forward_tables(count))
    row_table = jnp.asarray(row_tables(count, cells_y))
    params = pltpu.CompilerParams(vmem_limit_bytes=56 << 20)

    below = passed_along(density[-2:, middle:], "gx", 1)
    above = passed_along(density[:2, :middle], "gx", -1)
    packed = pl.pallas_call(
        functools.partial(pack_kernel, count),
        out_shape=jax.ShapeDtypeStruct((2 * terms + 1, count, 6 * lanes), f32),
        compiler_params=params,
        cost_estimate=pl.CostEstimate(flops=4 << 30, bytes_accessed=8 << 20, transcendentals=0),
        name="pack",
    )(
        jnp.asarray(mode_lanes(count)[None]),
        gains_a.reshape(-1, count),
        gains_b.reshape(-1, count),
        loss_rates.reshape(-1, count),
    )
    field_shape = jax.ShapeDtypeStruct((cells_x, rows, 5 * lanes), f32)
    rim_shape = jax.ShapeDtypeStruct((cells_x, 2, count, 3 * lanes), f32)
    modes_scratch = pltpu.VMEM((cells_x, rows, 6 * lanes), f32)
    points_scratch = pltpu.VMEM((cells_x, rows, 5 * lanes), f32)
    field, up, down = pl.pallas_call(
        functools.partial(first_kernel, count, rest, terms, cells_y),
        out_shape=(field_shape, rim_shape, rim_shape),
        scratch_shapes=[modes_scratch, points_scratch, pltpu.VMEM((2, count, density.shape[2]), f32)],
        compiler_params=params,
        name="first",
    )(
        density, below, above, packed, inverse, forward_table, row_table,
        jnp.asarray(weights.T.astype(np.float32)), jnp.asarray(fold),
    )
    y_below = passed_along(up, "gy", 1)
    y_above = passed_along(down, "gy", -1)
    return pl.pallas_call(
        functools.partial(second_kernel, count, rest, terms, cells_y),
        out_shape=jax.ShapeDtypeStruct(density.shape, f32),
        scratch_shapes=[points_scratch, modes_scratch, points_scratch],
        compiler_params=params,
        name="second",
    )(
        field, y_below, y_above, packed, inverse, forward_table, row_table,
        jnp.asarray(lane_speed), jnp.asarray(natural),
    )


def solution(mesh):
    in_specs = (P("gx", None, "gy"), P(), P(), P())
    out_specs = P("gx", None, "gy")
    return jax.shard_map(body, mesh=mesh, in_specs=in_specs, out_specs=out_specs, check_vma=False)
```

```python
import functools

import jax
import jax.numpy as jnp
import numpy as np
from jax import lax
from jax.experimental import pallas as pl
from jax.experimental.pallas import tpu as pltpu
from jax.sharding import PartitionSpec as P

courant_max = 1.6
collide_step = 0.2
lanes = 128
bf16 = jnp.bfloat16
f32 = jnp.float32
dot = functools.partial(jnp.dot, preferred_element_type=f32)


def passed_along(value, axis, steps):
    count = lax.axis_size(axis)
    pairs = [(source, (source + steps) % count) for source in range(count)]
    return lax.ppermute(value, axis, pairs)


def cosine_table(count):
    freq = np.arange(count)[:, None]
    points = np.arange(count)[None, :]
    scale = np.where(freq == 0, np.sqrt(1.0 / count), np.sqrt(2.0 / count))
    return scale * np.cos(np.pi * (2.0 * points + 1.0) * freq / (2.0 * count))


def two_parts(table):
    high = np.asarray(table, np.float32).astype(bf16)
    return high, (table - high.astype(np.float64)).astype(np.float32).astype(bf16)


def courant_weights(count):
    speeds = np.arange(count) - (count - 1) / 2.0
    a = courant_max * np.abs(speeds) / ((count - 1) / 2.0)
    return np.stack([1.0 - 1.5 * a + 0.5 * a * a, 2.0 * a - a * a, 0.5 * (a * a - a)])


def sign(s, q):
    return -1.0 if ((s >> 1) & (q >> 1)) ^ (s & 1 & q) else 1.0


def block_table(count, q):
    c = cosine_table(count)
    half = count // 2
    return np.kron(c[q >> 1 :: 2, :half], c[q & 1 :: 2, :half])


def point_lanes(count):
    half = count // 2
    block = half * half
    rest = block - lanes
    source = np.full(5 * lanes, -1, np.int32)
    for s in range(4):
        for m in range(block):
            j, l = divmod(m, half)
            y = count - 1 - j if s >> 1 else j
            z = count - 1 - l if s & 1 else l
            if m < lanes:
                source[s * lanes + m] = y * count + z
            else:
                for copy in range(2):
                    source[4 * lanes + copy * 4 * rest + s * rest + m - lanes] = y * count + z
    return source


def mode_lanes(count):
    half = count // 2
    block = half * half
    rest = block - lanes
    source = np.full(6 * lanes, -1, np.int32)
    for q in range(4):
        for m in range(block):
            j, l = divmod(m, half)
            place = (2 * j + (q >> 1)) * count + 2 * l + (q & 1)
            if m < lanes:
                source[q * lanes + m] = place
            else:
                for copy in range(3):
                    source[(4 + q // 2) * lanes + copy * 2 * rest + (q % 2) * rest + m - lanes] = place
    return source


def inverse_tables(count):
    rest = (count // 2) ** 2 - lanes
    out = np.zeros((4, 4 * lanes, 2 * lanes), bf16)
    for q in range(4):
        table = block_table(count, q)
        wide = np.zeros((table.shape[0], 2 * lanes))
        wide[:, :lanes] = table[:, :lanes]
        for s in range(4):
            for copy in range(2):
                at = lanes + copy * 4 * rest + s * rest
                wide[:, at : at + rest] = sign(s, q) * table[:, lanes:]
        high, low = two_parts(wide)
        out[q, :lanes] = high[:lanes]
        out[q, lanes : 2 * lanes] = high[:lanes]
        out[q, 2 * lanes : 3 * lanes] = low[:lanes]
        for copy, part in enumerate((high, high, low)):
            at = 3 * lanes + copy * 2 * rest + (q % 2) * rest
            out[q, at : at + rest] = part[lanes:]
    return out


def forward_tables(count):
    rest = (count // 2) ** 2 - lanes
    out = np.zeros((4, 5 * lanes, 2 * lanes), bf16)
    for q in range(4):
        table = block_table(count, q).T
        wide = np.zeros((table.shape[0], 2 * lanes))
        wide[:, :lanes] = table[:, :lanes]
        for copy in range(3):
            at = lanes + copy * 2 * rest + (q % 2) * rest
            wide[:, at : at + rest] = table[:, lanes:]
        high, low = two_parts(wide)
        out[q, :lanes] = high[:lanes]
        out[q, lanes : 2 * lanes] = high[:lanes]
        out[q, 2 * lanes : 3 * lanes] = low[:lanes]
        for s in range(4):
            for at, part in ((3 * lanes, high), (3 * lanes + 4 * rest, high), (4 * lanes, low)):
                at = at + s * rest
                out[q, at : at + rest] = (sign(s, q) * part[lanes:].astype(np.float32)).astype(bf16)
    return out


def row_groups(rows):
    middle = rows // 2
    return ((0, middle, 0, -(-middle // 16) * 16), (middle, rows, middle // 16 * 16, rows))


def row_tables(count, cells):
    c = cosine_table(count)
    result = []
    for table in (c, c.T):
        whole = np.kron(np.eye(cells), table)
        groups = []
        for first, last, low, high in row_groups(cells * count):
            coarse, fine = two_parts(whole[first:last, low:high])
            groups.append(np.concatenate([coarse, coarse, fine], axis=1))
        result.append(np.stack(groups))
    return np.stack(result)


def split(value):
    high = value.astype(bf16)
    return high, (value - high.astype(f32)).astype(bf16)


def lane_index():
    return lax.broadcasted_iota(jnp.int32, (1, lanes), 1)


def tile(value, at):
    return value[:, at * lanes : (at + 1) * lanes]


def crossed(v0, v1, v2, v3):
    t0, t1, t2, t3 = v0 + v1, v0 - v1, v2 + v3, v2 - v3
    return t0 + t2, t1 + t3, t0 - t2, t1 - t3


def along_rows(values, tables, rows):
    parts = [split(value) for value in values]
    found = []
    for g, (_, _, first, last) in enumerate(row_groups(rows)):
        pieces = [
            jnp.concatenate([high[first:last], low[first:last], high[first:last]], axis=0) for high, low in parts
        ]
        found.append(dot(tables[g], jnp.concatenate(pieces, axis=1)))
    return found


def forward(value, table_ref, rest):
    mixed = crossed(*[tile(value, s) for s in range(4)])
    high, low = split(tile(value, 4))
    both = jnp.where(lane_index() < 4 * rest, high.astype(f32), low.astype(f32)).astype(bf16)
    found = []
    for q in range(4):
        q_high, q_low = split(mixed[q])
        found.append(dot(jnp.concatenate([q_high, q_low, q_high, both, high], axis=1), table_ref[q]))
    return jnp.concatenate(
        [tile(v, 0) for v in found] + [tile(found[0], 1) + tile(found[1], 1), tile(found[2], 1) + tile(found[3], 1)],
        axis=1,
    )


def inverse_plane(modes, table_ref, rest):
    low_lanes = (lane_index() >= 2 * rest) & (lane_index() < 4 * rest)
    both = []
    for pair in range(2):
        value = tile(modes, 4 + pair)
        high = value.astype(bf16).astype(f32)
        both.append(jnp.where(low_lanes, value - high, high).astype(bf16))
    found = []
    for q in range(4):
        high, low = split(tile(modes, q))
        found.append(dot(jnp.concatenate([high, low, high, both[q // 2]], axis=1), table_ref[q]))
    main = crossed(*[tile(v, 0) for v in found])
    last = (tile(found[0], 1) + tile(found[1], 1)) + (tile(found[2], 1) + tile(found[3], 1))
    return jnp.concatenate(list(main) + [last], axis=1)


def collide(field_ref, modes_ref, sum_ref, kernel_ref, loss_ref, inverse_ref, forward_ref, rows_ref, count, rest):
    rows = field_ref.shape[0]
    cells = rows // count
    terms = kernel_ref.shape[0]
    together = 2 if terms % 2 == 0 else 1
    wide = 5 * lanes
    groups = [(first, last) for first, last, _, _ in row_groups(rows)]

    def scaled(factor):
        modes = modes_ref[...].reshape(cells, count, 6 * lanes)
        return (modes * factor[None]).reshape(rows, 6 * lanes)

    found = along_rows([forward(field_ref[...], forward_ref, rest)], rows_ref.at[0], rows)
    for (first, last), part in zip(groups, found):
        modes_ref[first:last] = part
    plane = inverse_plane(scaled(loss_ref[...]), inverse_ref, rest)
    found = along_rows([plane], rows_ref.at[1], rows)
    for (first, last), part in zip(groups, found):
        sum_ref[first:last] = -field_ref[first:last] * part

    def term(step, carry):
        factors = [kernel_ref[together * step + k, side] for k in range(together) for side in range(2)]
        plane = inverse_plane(jnp.concatenate([scaled(f) for f in factors], axis=0), inverse_ref, rest)
        planes = [plane[k * rows : (k + 1) * rows] for k in range(2 * together)]
        for (first, last), part in zip(groups, along_rows(planes, rows_ref.at[1], rows)):
            total = sum_ref[first:last]
            for k in range(together):
                at = 2 * k * wide
                total = total + part[:, at : at + wide] * part[:, at + wide : at + 2 * wide]
            sum_ref[first:last] = total
        return carry

    lax.fori_loop(0, terms // together, term, 0)
    field_ref[...] = field_ref[...] + collide_step * sum_ref[...]


def one_hot(source_row, rows):
    index = lax.broadcasted_iota(jnp.int32, (rows, source_row.shape[1]), 0)
    return jnp.where(index == source_row, 1.0, 0.0).astype(bf16)


def moved(value, table):
    high, low = split(value)
    return dot(high, table) + dot(low, table)


def pack_kernel(count, source_ref, a_ref, b_ref, loss_ref, out_ref, loss_out_ref, table_ref):
    @pl.when(pl.program_id(0) == 0)
    def _():
        table_ref[...] = one_hot(source_ref[...], count * count)

    def rows_of(ref):
        rows = ref.shape[0] // count
        return jnp.concatenate([ref[pl.ds(k, rows, stride=count), :] for k in range(count)], axis=1)

    terms = out_ref.shape[0]
    both = jnp.concatenate([rows_of(a_ref), rows_of(b_ref)], axis=0)
    both = moved(both, table_ref[...]).reshape(2, terms, count, 6 * lanes)
    for side in range(2):
        out_ref[:, side] = both[side]

    @pl.when(pl.program_id(0) == 0)
    def _():
        loss_out_ref[...] = moved(rows_of(loss_ref), table_ref[...])


class Half:
    def __init__(self, which, cells_x, cells_y, plane):
        first, last = which * cells_y // 2, (which + 1) * cells_y // 2
        self.cells = range(first, last)
        self.start = first * plane // lanes * lanes
        self.stop = -(-last * plane // lanes) * lanes
        self.shifts = [[y for y in self.cells if y * plane % lanes == shift] for shift in (0, lanes // 2)]
        self.order = [(x, y) for shift in self.shifts for x in range(cells_x) for y in shift]

    def rows(self, x, y, count):
        at = self.order.index((x, y)) * count
        return slice(at, at + count)

    def window(self, y, plane):
        return y * plane // lanes * lanes - self.start


def first_kernel(count, rest, halves, which, *refs):
    density_ref, below_ref, above_ref = refs[:3]
    refs = refs[3:]
    if which:
        earlier, refs = refs[:2], refs[2:]
    kernel_ref, loss_ref, inverse_ref, forward_ref, rows_ref, speed_ref, source_ref = refs[:7]
    out_ref, rim_out_ref, field_ref, modes_ref, sum_ref, rim_ref = refs[7:]
    half = halves[which]
    cells_x = density_ref.shape[0]
    middle = count // 2
    plane = count * count
    known = half.stop - half.start - below_ref.shape[2]
    for i in range(2):
        rim_ref[i, :middle, known:] = above_ref[i]
        rim_ref[i, middle:, known:] = below_ref[i]
        if known:
            rim_ref[i, :middle, :known] = earlier[1][i]
            rim_ref[i, middle:, :known] = earlier[0][i]
    positive = lax.broadcasted_iota(jnp.int32, (count, 1), 0) >= middle
    tables = [one_hot(source_ref[k : k + 1], 5 * lanes) for k in range(2)]

    def own(x):
        return density_ref[x, :, half.start : half.stop]

    def behind(x):
        return own(x) if x >= 0 else rim_ref[x + 2]

    def ahead(x):
        return own(x) if x < cells_x else rim_ref[x - cells_x]

    w0, w1, w2 = [speed_ref[:, k : k + 1] for k in range(3)]
    moved_on = []
    for x in range(cells_x):
        near = jnp.where(positive, behind(x - 1), ahead(x + 1))
        far = jnp.where(positive, behind(x - 2), ahead(x + 2))
        moved_on.append(w0 * own(x) + w1 * near + w2 * far)
    at = 0
    for k, shift in enumerate(half.shifts):
        parts = []
        for x in range(cells_x):
            for y in shift:
                window = half.window(y, plane)
                parts.append(moved_on[x][:, window : window + 5 * lanes])
        size = len(parts) * count
        field_ref[at : at + size] = moved(jnp.concatenate(parts, axis=0), tables[k])
        at += size
    collide(field_ref, modes_ref, sum_ref, kernel_ref, loss_ref, inverse_ref, forward_ref, rows_ref, count, rest)
    out_ref[...] = field_ref[...]
    for x in range(cells_x):
        for k in range(2):
            if which:
                rim_out_ref[x, k] = field_ref[half.rows(x, half.cells[k - 2], count), 2 * lanes :]
            else:
                at = half.rows(x, half.cells[k], count)
                rim_out_ref[x, k, :, : 2 * lanes] = field_ref[at, : 2 * lanes]
                rim_out_ref[x, k, :, 2 * lanes :] = field_ref[at, 4 * lanes :]


def second_kernel(count, rest, halves, which, *refs):
    given = refs[:2]
    rim_ref, kernel_ref, loss_ref, inverse_ref, forward_ref, rows_ref, speed_ref, source_ref = refs[2:10]
    refs = refs[10:]
    if not which:
        upper_ref, refs = refs[0], refs[1:]
    out_ref, field_ref, modes_ref, sum_ref = refs
    half = halves[which]
    cells_x = rim_ref.shape[0]
    cells_y = halves[1].cells[-1] + 1
    plane = count * count
    backward_last = (lane_index() // (2 * rest)) % 2 == 1

    def cell(x, y, part):
        if y < 0:
            return rim_ref[x, y + 2, :, (part - 2) * lanes : (part - 1) * lanes]
        if y >= cells_y:
            at = part if part < 2 else 2
            return rim_ref[x, y - cells_y, :, at * lanes : (at + 1) * lanes]
        place = 0 if y in halves[0].cells else 1
        return given[place][halves[place].rows(x, y, count), part * lanes : (part + 1) * lanes]

    for x, y in half.order:
        for part in range(5):
            w0, w1, w2 = [speed_ref[k : k + 1, part * lanes : (part + 1) * lanes] for k in range(3)]
            if part < 2:
                near, far = cell(x, y + 1, part), cell(x, y + 2, part)
            elif part < 4:
                near, far = cell(x, y - 1, part), cell(x, y - 2, part)
            else:
                near = jnp.where(backward_last, cell(x, y - 1, part), cell(x, y + 1, part))
                far = jnp.where(backward_last, cell(x, y - 2, part), cell(x, y + 2, part))
            field_ref[half.rows(x, y, count), part * lanes : (part + 1) * lanes] = (
                w0 * cell(x, y, part) + w1 * near + w2 * far
            )
    collide(field_ref, modes_ref, sum_ref, kernel_ref, loss_ref, inverse_ref, forward_ref, rows_ref, count, rest)
    at = 0
    pieces = {}
    for k, shift in enumerate(half.shifts):
        cells = [(x, y) for x in range(cells_x) for y in shift]
        size = len(cells) * count
        natural = moved(field_ref[at : at + size], one_hot(source_ref[k : k + 1], 5 * lanes))
        at += size
        for i, place in enumerate(cells):
            pieces[place] = natural[i * count : (i + 1) * count]
    for x in range(cells_x):
        filled = {}
        for y in half.cells:
            window = half.window(y, plane) // lanes
            for t in range(5):
                value = tile(pieces[x, y], t)
                filled[window + t] = filled[window + t] + value if window + t in filled else value
        shared = 0
        if not which:
            shared = halves[1].start // lanes
            for t in range(shared, halves[1].stop // lanes):
                value = upper_ref[x, :, (t - shared) * lanes : (t - shared + 1) * lanes]
                filled[t] = filled[t] + value if t in filled else value
        for t, value in filled.items():
            out_ref[x, :, t * lanes : (t + 1) * lanes] = value


def body(density, gains_a, gains_b, loss_rates):
    cells_x, count, width = density.shape
    terms = gains_a.shape[0]
    middle = count // 2
    plane = count * count
    cells_y = width // plane
    rest = middle * middle - lanes
    halves = [Half(which, cells_x, cells_y, plane) for which in range(2)]
    rows = len(halves[0].order) * count
    points = point_lanes(count)
    natural = np.full((2, 5 * lanes), -1, np.int32)
    for lane in range(4 * lanes + 4 * rest):
        natural[0, points[lane]] = lane
        natural[1, points[lane] + lanes // 2] = lane
    fold = np.where(points >= 0, np.stack([points, points + lanes // 2]), -1).astype(np.int32)
    weights = courant_weights(count)
    lane_speed = np.where(points >= 0, weights[:, points // count], 0.0).astype(np.float32)
    tables = [jnp.asarray(t) for t in (inverse_tables(count), forward_tables(count), row_tables(count, rows // count))]
    row_speed = jnp.asarray(weights.T.astype(np.float32))
    params = pltpu.CompilerParams(vmem_limit_bytes=56 << 20)
    cost = pl.CostEstimate(flops=10 << 30, bytes_accessed=4 << 20, transcendentals=0)
    whole = pl.BlockSpec(memory_space=pltpu.VMEM)

    cut = halves[0].stop
    rims = []
    for first, last in ((0, cut), (cut, width)):
        rims.append(
            (
                passed_along(density[-2:, middle:, first:last], "gx", 1),
                passed_along(density[:2, :middle, first:last], "gx", -1),
            )
        )
    steps = 4 if terms % 4 == 0 else 1
    taken = terms // steps
    gain_spec = pl.BlockSpec((taken * plane, count), lambda i: (i, 0))
    packed, packed_loss = pl.pallas_call(
        functools.partial(pack_kernel, count),
        grid=(steps,),
        in_specs=[
            pl.BlockSpec((1, 6 * lanes), lambda i: (0, 0)),
            gain_spec,
            gain_spec,
            pl.BlockSpec((plane, count), lambda i: (0, 0)),
        ],
        out_specs=[
            pl.BlockSpec((taken, 2, count, 6 * lanes), lambda i: (i, 0, 0, 0)),
            pl.BlockSpec((count, 6 * lanes), lambda i: (0, 0)),
        ],
        out_shape=(
            jax.ShapeDtypeStruct((terms, 2, count, 6 * lanes), f32),
            jax.ShapeDtypeStruct((count, 6 * lanes), f32),
        ),
        scratch_shapes=[pltpu.VMEM((plane, 6 * lanes), bf16)],
        compiler_params=params,
        cost_estimate=pl.CostEstimate(flops=4 << 30, bytes_accessed=8 << 20, transcendentals=0),
        name="pack",
    )(
        jnp.asarray(mode_lanes(count)[None]),
        gains_a.reshape(-1, count),
        gains_b.reshape(-1, count),
        loss_rates.reshape(-1, count),
    )
    field_shape = jax.ShapeDtypeStruct((rows, 5 * lanes), f32)
    rim_shape = jax.ShapeDtypeStruct((cells_x, 2, count, 3 * lanes), f32)
    scratch = [pltpu.VMEM((rows, k * lanes), f32) for k in (5, 6, 5)]
    fields = []
    y_rims = []
    for which, half in enumerate(halves):
        known = half.stop - half.start - rims[which][0].shape[2]
        edge = pl.BlockSpec((2, middle, max(known, 1)), lambda i, at=halves[1].start // max(known, 1): (0, 0, at))
        field, rim = pl.pallas_call(
            functools.partial(first_kernel, count, rest, halves, which),
            grid=(1,) if which else (),
            in_specs=[whole] * 3 + [edge] * (2 * which) + [whole] * 7,
            out_shape=(field_shape, rim_shape),
            scratch_shapes=scratch + [pltpu.VMEM((2, count, half.stop - half.start), f32)],
            compiler_params=params,
            cost_estimate=cost,
            name=f"first_{which}",
        )(
            density, *rims[which], *(rims[0] if which else ()), packed, packed_loss, *tables, row_speed,
            jnp.asarray(fold),
        )
        fields.append(field)
        y_rims.append(passed_along(rim, "gy", 1 if which else -1))
    result = ()
    for which in (1, 0):
        shape = density.shape if not which else (cells_x, count, halves[1].stop - halves[1].start)
        result = (
            pl.pallas_call(
                functools.partial(second_kernel, count, rest, halves, which),
                out_shape=jax.ShapeDtypeStruct(shape, f32),
                scratch_shapes=scratch,
                compiler_params=params,
                cost_estimate=cost,
                name=f"second_{which}",
            )(
                *fields, y_rims[1 - which], packed, packed_loss, *tables, jnp.asarray(lane_speed),
                jnp.asarray(natural), *result,
            ),
        )
    return result[0]


def solution(mesh):
    in_specs = (P("gx", None, "gy"), P(), P(), P())
    out_specs = P("gx", None, "gy")
    return jax.shard_map(body, mesh=mesh, in_specs=in_specs, out_specs=out_specs, check_vma=False)
```

```python
import functools

import jax
import jax.numpy as jnp
import numpy as np
from jax import lax
from jax.experimental import pallas as pl
from jax.experimental.pallas import tpu as pltpu
from jax.sharding import PartitionSpec as P

courant_max = 1.6
collide_step = 0.2
lanes = 128
pack_mib, first_mib, second_mib = 24, 28, 24
bf16 = jnp.bfloat16
f32 = jnp.float32
dot = functools.partial(jnp.dot, preferred_element_type=f32)


def passed_along(value, axis, steps):
    count = lax.axis_size(axis)
    pairs = [(source, (source + steps) % count) for source in range(count)]
    return lax.ppermute(value, axis, pairs)


def cosine_table(count):
    freq = np.arange(count)[:, None]
    points = np.arange(count)[None, :]
    scale = np.where(freq == 0, np.sqrt(1.0 / count), np.sqrt(2.0 / count))
    return scale * np.cos(np.pi * (2.0 * points + 1.0) * freq / (2.0 * count))


def two_parts(table):
    high = np.asarray(table, np.float32).astype(bf16)
    return high, (table - high.astype(np.float64)).astype(np.float32).astype(bf16)


def courant_weights(count):
    speeds = np.arange(count) - (count - 1) / 2.0
    a = courant_max * np.abs(speeds) / ((count - 1) / 2.0)
    return np.stack([1.0 - 1.5 * a + 0.5 * a * a, 2.0 * a - a * a, 0.5 * (a * a - a)])


def sign(s, q):
    return -1.0 if ((s >> 1) & (q >> 1)) ^ (s & 1 & q) else 1.0


def block_table(count, q):
    c = cosine_table(count)
    half = count // 2
    return np.kron(c[q >> 1 :: 2, :half], c[q & 1 :: 2, :half])


def point_lanes(count):
    half = count // 2
    block = half * half
    rest = block - lanes
    source = np.full(5 * lanes, -1, np.int32)
    for s in range(4):
        for m in range(block):
            j, l = divmod(m, half)
            y = count - 1 - j if s >> 1 else j
            z = count - 1 - l if s & 1 else l
            if m < lanes:
                source[s * lanes + m] = y * count + z
            else:
                for copy in range(2):
                    source[4 * lanes + copy * 4 * rest + s * rest + m - lanes] = y * count + z
    return source


def mode_lanes(count):
    half = count // 2
    block = half * half
    rest = block - lanes
    source = np.full(6 * lanes, -1, np.int32)
    for q in range(4):
        for m in range(block):
            j, l = divmod(m, half)
            place = (2 * j + (q >> 1)) * count + 2 * l + (q & 1)
            if m < lanes:
                source[q * lanes + m] = place
            else:
                for copy in range(3):
                    source[(4 + q // 2) * lanes + copy * 2 * rest + (q % 2) * rest + m - lanes] = place
    return source


def inverse_tables(count):
    rest = (count // 2) ** 2 - lanes
    out = np.zeros((4, 4 * lanes, 2 * lanes), bf16)
    for q in range(4):
        table = block_table(count, q)
        wide = np.zeros((table.shape[0], 2 * lanes))
        wide[:, :lanes] = table[:, :lanes]
        for s in range(4):
            for copy in range(2):
                at = lanes + copy * 4 * rest + s * rest
                wide[:, at : at + rest] = sign(s, q) * table[:, lanes:]
        high, low = two_parts(wide)
        out[q, :lanes] = high[:lanes]
        out[q, lanes : 2 * lanes] = high[:lanes]
        out[q, 2 * lanes : 3 * lanes] = low[:lanes]
        for copy, part in enumerate((high, high, low)):
            at = 3 * lanes + copy * 2 * rest + (q % 2) * rest
            out[q, at : at + rest] = part[lanes:]
    return out


def forward_tables(count):
    rest = (count // 2) ** 2 - lanes
    out = np.zeros((4, 5 * lanes, 2 * lanes), bf16)
    for q in range(4):
        table = block_table(count, q).T
        wide = np.zeros((table.shape[0], 2 * lanes))
        wide[:, :lanes] = table[:, :lanes]
        for copy in range(3):
            at = lanes + copy * 2 * rest + (q % 2) * rest
            wide[:, at : at + rest] = table[:, lanes:]
        high, low = two_parts(wide)
        out[q, :lanes] = high[:lanes]
        out[q, lanes : 2 * lanes] = high[:lanes]
        out[q, 2 * lanes : 3 * lanes] = low[:lanes]
        for s in range(4):
            for at, part in ((3 * lanes, high), (3 * lanes + 4 * rest, high), (4 * lanes, low)):
                at = at + s * rest
                out[q, at : at + rest] = (sign(s, q) * part[lanes:].astype(np.float32)).astype(bf16)
    return out


def cells_together(cells):
    return max(n for n in (1, 2, 4) if cells % n == 0)


def row_tables(count, cells):
    c = cosine_table(count)
    result = []
    for table in (c, c.T):
        coarse, fine = two_parts(np.kron(np.eye(cells), table))
        upper = np.concatenate([coarse, coarse], axis=1)
        lower = np.concatenate([fine, np.zeros_like(fine)], axis=1)
        result.append(np.concatenate([upper, lower], axis=0))
    return np.stack(result)


def split(value):
    high = value.astype(bf16)
    return high, (value - high.astype(f32)).astype(bf16)


def lane_index():
    return lax.broadcasted_iota(jnp.int32, (1, lanes), 1)


def tile(value, at):
    return value[:, at * lanes : (at + 1) * lanes]


def crossed(v0, v1, v2, v3):
    t0, t1, t2, t3 = v0 + v1, v0 - v1, v2 + v3, v2 - v3
    return t0 + t2, t1 + t3, t0 - t2, t1 - t3


def along_rows(values, table, size):
    parts = [split(value) for value in values]
    found = []
    for at in range(0, values[0].shape[0], size):
        pieces = [jnp.concatenate([high[at : at + size], low[at : at + size]], axis=0) for high, low in parts]
        both = dot(table, jnp.concatenate(pieces, axis=1))
        found.append(both[:size] + both[size:])
    return found


def forward(value, table_ref, rest):
    mixed = crossed(*[tile(value, s) for s in range(4)])
    high, low = split(tile(value, 4))
    both = jnp.where(lane_index() < 4 * rest, high.astype(f32), low.astype(f32)).astype(bf16)
    found = []
    for q in range(4):
        q_high, q_low = split(mixed[q])
        found.append(dot(jnp.concatenate([q_high, q_low, q_high, both, high], axis=1), table_ref[q]))
    return jnp.concatenate(
        [tile(v, 0) for v in found] + [tile(found[0], 1) + tile(found[1], 1), tile(found[2], 1) + tile(found[3], 1)],
        axis=1,
    )


def inverse_plane(modes, table_ref, rest):
    low_lanes = (lane_index() >= 2 * rest) & (lane_index() < 4 * rest)
    both = []
    for pair in range(2):
        value = tile(modes, 4 + pair)
        high = value.astype(bf16).astype(f32)
        both.append(jnp.where(low_lanes, value - high, high).astype(bf16))
    found = []
    for q in range(4):
        high, low = split(tile(modes, q))
        found.append(dot(jnp.concatenate([high, low, high, both[q // 2]], axis=1), table_ref[q]))
    main = crossed(*[tile(v, 0) for v in found])
    last = (tile(found[0], 1) + tile(found[1], 1)) + (tile(found[2], 1) + tile(found[3], 1))
    return jnp.concatenate(list(main) + [last], axis=1)


def collide(field_ref, modes_ref, sum_ref, kernel_ref, loss_ref, inverse_ref, forward_ref, rows_ref, count, rest, most):
    rows = field_ref.shape[0]
    cells = rows // count
    terms = kernel_ref.shape[0]
    together = max(n for n in range(1, most + 1) if terms % n == 0)
    wide = 5 * lanes
    size = rows_ref.shape[2] // 2

    def scaled(factor):
        modes = modes_ref[...].reshape(cells, count, 6 * lanes)
        return (modes * factor[None]).reshape(rows, 6 * lanes)

    for k, part in enumerate(along_rows([forward(field_ref[...], forward_ref, rest)], rows_ref[0], size)):
        modes_ref[k * size : (k + 1) * size] = part
    plane = inverse_plane(scaled(loss_ref[...]), inverse_ref, rest)
    for k, part in enumerate(along_rows([plane], rows_ref[1], size)):
        at = slice(k * size, (k + 1) * size)
        sum_ref[at] = -field_ref[at] * part

    def term(step, carry):
        factors = [kernel_ref[together * step + k, side] for k in range(together) for side in range(2)]
        plane = inverse_plane(jnp.concatenate([scaled(f) for f in factors], axis=0), inverse_ref, rest)
        planes = [plane[k * rows : (k + 1) * rows] for k in range(2 * together)]
        for k, part in enumerate(along_rows(planes, rows_ref[1], size)):
            at = slice(k * size, (k + 1) * size)
            total = sum_ref[at]
            for pair in range(together):
                lane = 2 * pair * wide
                total = total + part[:, lane : lane + wide] * part[:, lane + wide : lane + 2 * wide]
            sum_ref[at] = total
        return carry

    lax.fori_loop(0, terms // together, term, 0)
    field_ref[...] = field_ref[...] + collide_step * sum_ref[...]


def one_hot(source_row, rows):
    index = lax.broadcasted_iota(jnp.int32, (rows, source_row.shape[1]), 0)
    return jnp.where(index == source_row, 1.0, 0.0).astype(bf16)


def moved(value, table):
    high, low = split(value)
    both = dot(jnp.concatenate([high, low], axis=0), table)
    return both[: value.shape[0]] + both[value.shape[0] :]


def pack_kernel(count, source_ref, move_ref, a_ref, b_ref, loss_ref, out_ref, loss_out_ref, moves_ref, table_ref):
    @pl.when(pl.program_id(0) == 0)
    def _():
        table_ref[...] = one_hot(source_ref[...], count * count)

    for k in range(moves_ref.shape[0]):
        moves_ref[k] = one_hot(move_ref[k], 5 * lanes)

    def rows_of(ref):
        rows = ref.shape[0] // count
        return jnp.concatenate([ref[pl.ds(k, rows, stride=count), :] for k in range(count)], axis=1)

    terms = out_ref.shape[0]
    both = jnp.concatenate([rows_of(a_ref), rows_of(b_ref)], axis=0)
    both = moved(both, table_ref[...]).reshape(2, terms, count, 6 * lanes)
    for side in range(2):
        out_ref[:, side] = both[side]

    @pl.when(pl.program_id(0) == 0)
    def _():
        loss_out_ref[...] = moved(rows_of(loss_ref), table_ref[...])


class Cells:
    def __init__(self, cells_x, count, ys):
        plane = count * count
        self.count = count
        self.parts = [
            [(x, y) for x in range(cells_x) for y in ys if y * plane % lanes == shift] for shift in (0, lanes // 2)
        ]
        self.order = self.parts[0] + self.parts[1]
        self.size = len(self.order) * count

    def rows(self, x, y):
        at = self.order.index((x, y)) * self.count
        return slice(at, at + self.count)

    def part_rows(self, k):
        at = k * len(self.parts[0]) * self.count
        return slice(at, at + len(self.parts[k]) * self.count)


def first_kernel(
    count, rest, cells, cells_y,
    density_ref, below_ref, above_ref, kernel_ref, loss_ref, inverse_ref, forward_ref, rows_ref, speed_ref, moves_ref,
    field_ref, up_ref, down_ref, modes_ref, sum_ref, rim_ref,
):
    cells_x = density_ref.shape[0]
    middle = count // 2
    plane = count * count
    for i in range(2):
        rim_ref[i, :middle] = above_ref[i]
        rim_ref[i, middle:] = below_ref[i]
    positive = lax.broadcasted_iota(jnp.int32, (count, 1), 0) >= middle

    def behind(x):
        return density_ref[x] if x >= 0 else rim_ref[x + 2]

    def ahead(x):
        return density_ref[x] if x < cells_x else rim_ref[x - cells_x]

    w0, w1, w2 = [speed_ref[:, k : k + 1] for k in range(3)]
    moved_on = []
    for x in range(cells_x):
        near = jnp.where(positive, behind(x - 1), ahead(x + 1))
        far = jnp.where(positive, behind(x - 2), ahead(x + 2))
        moved_on.append(w0 * density_ref[x] + w1 * near + w2 * far)
    for k, part in enumerate(cells.parts):
        starts = [(x, y * plane // lanes * lanes) for x, y in part]
        values = jnp.concatenate([moved_on[x][:, at : at + 5 * lanes] for x, at in starts], axis=0)
        field_ref[cells.part_rows(k)] = moved(values, moves_ref[k])
    collide(field_ref, modes_ref, sum_ref, kernel_ref, loss_ref, inverse_ref, forward_ref, rows_ref, count, rest, 2)
    for x in range(cells_x):
        for k in range(2):
            up_ref[x, k] = field_ref[cells.rows(x, cells_y - 2 + k), 2 * lanes :]
            down_ref[x, k, :, : 2 * lanes] = field_ref[cells.rows(x, k), : 2 * lanes]
            down_ref[x, k, :, 2 * lanes :] = field_ref[cells.rows(x, k), 4 * lanes :]


def sweep_y(given_ref, below_ref, above_ref, speed_ref, field_ref, everything, cells, cells_y, rest):
    backward_last = (lane_index() // (2 * rest)) % 2 == 1

    def cell(x, y, part):
        if y < 0:
            return below_ref[x, y + 2, :, (part - 2) * lanes : (part - 1) * lanes]
        if y >= cells_y:
            at = part if part < 2 else 2
            return above_ref[x, y - cells_y, :, at * lanes : (at + 1) * lanes]
        return given_ref[everything.rows(x, y), part * lanes : (part + 1) * lanes]

    for x, y in cells.order:
        for part in range(5):
            w0, w1, w2 = [speed_ref[k : k + 1, part * lanes : (part + 1) * lanes] for k in range(3)]
            if part < 2:
                near, far = cell(x, y + 1, part), cell(x, y + 2, part)
            elif part < 4:
                near, far = cell(x, y - 1, part), cell(x, y - 2, part)
            else:
                near = jnp.where(backward_last, cell(x, y - 1, part), cell(x, y + 1, part))
                far = jnp.where(backward_last, cell(x, y - 2, part), cell(x, y + 2, part))
            field_ref[cells.rows(x, y), part * lanes : (part + 1) * lanes] = (
                w0 * cell(x, y, part) + w1 * near + w2 * far
            )


def inner_kernel(
    count, rest, everything, cells, cells_y,
    given_ref, kernel_ref, loss_ref, inverse_ref, forward_ref, rows_ref, speed_ref,
    field_ref, modes_ref, sum_ref,
):
    sweep_y(given_ref, None, None, speed_ref, field_ref, everything, cells, cells_y, rest)
    collide(field_ref, modes_ref, sum_ref, kernel_ref, loss_ref, inverse_ref, forward_ref, rows_ref, count, rest, 4)


def outer_kernel(
    count, rest, everything, inner, cells, cells_y,
    given_ref, inner_ref, below_ref, above_ref, kernel_ref, loss_ref, inverse_ref, forward_ref, rows_ref, speed_ref,
    moves_ref,
    out_ref, field_ref, modes_ref, sum_ref,
):
    plane = count * count
    sweep_y(given_ref, below_ref, above_ref, speed_ref, field_ref, everything, cells, cells_y, rest)
    collide(field_ref, modes_ref, sum_ref, kernel_ref, loss_ref, inverse_ref, forward_ref, rows_ref, count, rest, 2)
    pieces = {}
    for k in range(2):
        values = [field_ref[cells.part_rows(k)], inner_ref[inner.part_rows(k)]]
        natural = moved(jnp.concatenate(values, axis=0), moves_ref[2 + k])
        for i, place in enumerate(cells.parts[k] + inner.parts[k]):
            pieces[place] = natural[i * count : (i + 1) * count]
    for x in range(out_ref.shape[0]):
        filled = {}
        for y in range(cells_y):
            first = y * plane // lanes
            for t in range(5):
                value = tile(pieces[x, y], t)
                filled[first + t] = filled[first + t] + value if first + t in filled else value
        for t in range(out_ref.shape[2] // lanes):
            out_ref[x, :, t * lanes : (t + 1) * lanes] = filled[t]


def body(density, gains_a, gains_b, loss_rates):
    cells_x, count, width = density.shape
    terms = gains_a.shape[0]
    middle = count // 2
    plane = count * count
    cells_y = width // plane
    rest = middle * middle - lanes
    everything = Cells(cells_x, count, range(cells_y))
    inner = Cells(cells_x, count, range(2, cells_y - 2))
    outer = Cells(cells_x, count, [*range(2), *range(cells_y - 2, cells_y)])
    points = point_lanes(count)
    moves = np.full((4, 1, 5 * lanes), -1, np.int32)
    for k in range(2):
        shift = k * lanes // 2
        moves[k, 0] = np.where(points >= 0, points + shift, -1)
        for lane in range(4 * lanes + 4 * rest):
            moves[2 + k, 0, points[lane] + shift] = lane
    weights = courant_weights(count)
    lane_speed = np.where(points >= 0, weights[:, points // count], 0.0).astype(np.float32)
    lane_speed = jnp.asarray(lane_speed)
    row_speed = jnp.asarray(weights.T.astype(np.float32))
    group = min(cells_together(c.size // count) for c in (everything, inner, outer))
    tables = [jnp.asarray(t) for t in (inverse_tables(count), forward_tables(count), row_tables(count, group))]

    def params(mib):
        return pltpu.CompilerParams(vmem_limit_bytes=mib << 20)

    def scratch(cells):
        return [pltpu.VMEM((cells.size, k * lanes), f32) for k in (6, 5)]

    def cost(cells):
        return pl.CostEstimate(flops=cells.size << 27, bytes_accessed=4 << 20, transcendentals=0)

    below = passed_along(density[-2:, middle:], "gx", 1)
    above = passed_along(density[:2, :middle], "gx", -1)
    steps = 2 if terms % 2 == 0 else 1
    taken = terms // steps
    gain_spec = pl.BlockSpec((taken * plane, count), lambda i: (i, 0))
    packed, packed_loss, move_tables = pl.pallas_call(
        functools.partial(pack_kernel, count),
        grid=(steps,),
        in_specs=[
            pl.BlockSpec((1, 6 * lanes), lambda i: (0, 0)),
            pl.BlockSpec((4 // steps, 1, 5 * lanes), lambda i: (i, 0, 0)),
            gain_spec,
            gain_spec,
            pl.BlockSpec((plane, count), lambda i: (0, 0)),
        ],
        out_specs=[
            pl.BlockSpec((taken, 2, count, 6 * lanes), lambda i: (i, 0, 0, 0)),
            pl.BlockSpec((count, 6 * lanes), lambda i: (0, 0)),
            pl.BlockSpec((4 // steps, 5 * lanes, 5 * lanes), lambda i: (i, 0, 0)),
        ],
        out_shape=(
            jax.ShapeDtypeStruct((terms, 2, count, 6 * lanes), f32),
            jax.ShapeDtypeStruct((count, 6 * lanes), f32),
            jax.ShapeDtypeStruct((4, 5 * lanes, 5 * lanes), bf16),
        ),
        scratch_shapes=[pltpu.VMEM((plane, 6 * lanes), bf16)],
        compiler_params=params(pack_mib),
        cost_estimate=pl.CostEstimate(flops=4 << 30, bytes_accessed=8 << 20, transcendentals=0),
        name="pack",
    )(
        jnp.asarray(mode_lanes(count)[None]),
        jnp.asarray(moves),
        gains_a.reshape(-1, count),
        gains_b.reshape(-1, count),
        loss_rates.reshape(-1, count),
    )
    rim_shape = jax.ShapeDtypeStruct((cells_x, 2, count, 3 * lanes), f32)
    field, up, down = pl.pallas_call(
        functools.partial(first_kernel, count, rest, everything, cells_y),
        out_shape=(jax.ShapeDtypeStruct((everything.size, 5 * lanes), f32), rim_shape, rim_shape),
        scratch_shapes=scratch(everything) + [pltpu.VMEM((2, count, width), f32)],
        compiler_params=params(first_mib),
        cost_estimate=cost(everything),
        name="first",
    )(density, below, above, packed, packed_loss, *tables, row_speed, move_tables)
    y_below = passed_along(up, "gy", 1)
    y_above = passed_along(down, "gy", -1)
    inner_field = pl.pallas_call(
        functools.partial(inner_kernel, count, rest, everything, inner, cells_y),
        out_shape=jax.ShapeDtypeStruct((inner.size, 5 * lanes), f32),
        scratch_shapes=scratch(inner),
        compiler_params=params(second_mib),
        cost_estimate=cost(inner),
        name="inner",
    )(field, packed, packed_loss, *tables, lane_speed)
    return pl.pallas_call(
        functools.partial(outer_kernel, count, rest, everything, inner, outer, cells_y),
        out_shape=jax.ShapeDtypeStruct(density.shape, f32),
        scratch_shapes=[pltpu.VMEM((outer.size, 5 * lanes), f32)] + scratch(outer),
        compiler_params=params(second_mib),
        cost_estimate=cost(outer),
        name="outer",
    )(field, inner_field, y_below, y_above, packed, packed_loss, *tables, lane_speed, move_tables)


def solution(mesh):
    in_specs = (P("gx", None, "gy"), P(), P(), P())
    out_specs = P("gx", None, "gy")
    return jax.shard_map(body, mesh=mesh, in_specs=in_specs, out_specs=out_specs, check_vma=False)
```

```python
import functools

import jax
import jax.numpy as jnp
import numpy as np
from jax import lax
from jax.experimental import pallas as pl
from jax.experimental.pallas import tpu as pltpu
from jax.sharding import PartitionSpec as P

courant_max = 1.6
collide_step = 0.2
lanes = 128
pack_mib, first_mib, second_mib = 24, 28, 24
bf16 = jnp.bfloat16
f32 = jnp.float32
dot = functools.partial(jnp.dot, preferred_element_type=f32)


def passed_along(value, axis, steps):
    count = lax.axis_size(axis)
    pairs = [(source, (source + steps) % count) for source in range(count)]
    return lax.ppermute(value, axis, pairs)


def cosine_table(count):
    freq = np.arange(count)[:, None]
    points = np.arange(count)[None, :]
    scale = np.where(freq == 0, np.sqrt(1.0 / count), np.sqrt(2.0 / count))
    return scale * np.cos(np.pi * (2.0 * points + 1.0) * freq / (2.0 * count))


def two_parts(table):
    high = np.asarray(table, np.float32).astype(bf16)
    return high, (table - high.astype(np.float64)).astype(np.float32).astype(bf16)


def courant_weights(count):
    speeds = np.arange(count) - (count - 1) / 2.0
    a = courant_max * np.abs(speeds) / ((count - 1) / 2.0)
    return np.stack([1.0 - 1.5 * a + 0.5 * a * a, 2.0 * a - a * a, 0.5 * (a * a - a)])


def sign(s, q):
    return -1.0 if ((s >> 1) & (q >> 1)) ^ (s & 1 & q) else 1.0


def block_table(count, q):
    c = cosine_table(count)
    half = count // 2
    return np.kron(c[q >> 1 :: 2, :half], c[q & 1 :: 2, :half])


def point_lanes(count):
    half = count // 2
    block = half * half
    rest = block - lanes
    source = np.full(5 * lanes, -1, np.int32)
    for s in range(4):
        for m in range(block):
            j, l = divmod(m, half)
            y = count - 1 - j if s >> 1 else j
            z = count - 1 - l if s & 1 else l
            if m < lanes:
                source[s * lanes + m] = y * count + z
            else:
                for copy in range(2):
                    source[4 * lanes + copy * 4 * rest + s * rest + m - lanes] = y * count + z
    return source


def mode_lanes(count):
    half = count // 2
    block = half * half
    rest = block - lanes
    source = np.full(6 * lanes, -1, np.int32)
    for q in range(4):
        for m in range(block):
            j, l = divmod(m, half)
            place = (2 * j + (q >> 1)) * count + 2 * l + (q & 1)
            if m < lanes:
                source[q * lanes + m] = place
            else:
                for copy in range(3):
                    source[(4 + q // 2) * lanes + copy * 2 * rest + (q % 2) * rest + m - lanes] = place
    return source


def inverse_tables(count):
    rest = (count // 2) ** 2 - lanes
    out = np.zeros((4, 4 * lanes, 2 * lanes), bf16)
    for q in range(4):
        table = block_table(count, q)
        wide = np.zeros((table.shape[0], 2 * lanes))
        wide[:, :lanes] = table[:, :lanes]
        for s in range(4):
            for copy in range(2):
                at = lanes + copy * 4 * rest + s * rest
                wide[:, at : at + rest] = sign(s, q) * table[:, lanes:]
        high, low = two_parts(wide)
        out[q, :lanes] = high[:lanes]
        out[q, lanes : 2 * lanes] = high[:lanes]
        out[q, 2 * lanes : 3 * lanes] = low[:lanes]
        for copy, part in enumerate((high, high, low)):
            at = 3 * lanes + copy * 2 * rest + (q % 2) * rest
            out[q, at : at + rest] = part[lanes:]
    return out


def forward_tables(count):
    rest = (count // 2) ** 2 - lanes
    out = np.zeros((4, 5 * lanes, 2 * lanes), bf16)
    for q in range(4):
        table = block_table(count, q).T
        wide = np.zeros((table.shape[0], 2 * lanes))
        wide[:, :lanes] = table[:, :lanes]
        for copy in range(3):
            at = lanes + copy * 2 * rest + (q % 2) * rest
            wide[:, at : at + rest] = table[:, lanes:]
        high, low = two_parts(wide)
        out[q, :lanes] = high[:lanes]
        out[q, lanes : 2 * lanes] = high[:lanes]
        out[q, 2 * lanes : 3 * lanes] = low[:lanes]
        for s in range(4):
            for at, part in ((3 * lanes, high), (3 * lanes + 4 * rest, high), (4 * lanes, low)):
                at = at + s * rest
                out[q, at : at + rest] = (sign(s, q) * part[lanes:].astype(np.float32)).astype(bf16)
    return out


def cells_together(cells):
    return max(n for n in (1, 2, 4) if cells % n == 0)


def row_tables(count, cells):
    c = cosine_table(count)
    result = []
    for table in (c, c.T):
        coarse, fine = two_parts(np.kron(np.eye(cells), table))
        upper = np.concatenate([coarse, coarse], axis=1)
        lower = np.concatenate([fine, np.zeros_like(fine)], axis=1)
        result.append(np.concatenate([upper, lower], axis=0))
    return np.stack(result)


def split(value):
    high = value.astype(bf16)
    return high, (value - high.astype(f32)).astype(bf16)


def lane_index():
    return lax.broadcasted_iota(jnp.int32, (1, lanes), 1)


def tile(value, at):
    return value[:, at * lanes : (at + 1) * lanes]


def crossed(v0, v1, v2, v3):
    t0, t1, t2, t3 = v0 + v1, v0 - v1, v2 + v3, v2 - v3
    return t0 + t2, t1 + t3, t0 - t2, t1 - t3


def along_rows(values, table, size):
    parts = [split(value) for value in values]
    found = []
    for at in range(0, values[0].shape[0], size):
        pieces = [jnp.concatenate([high[at : at + size], low[at : at + size]], axis=0) for high, low in parts]
        both = dot(table, jnp.concatenate(pieces, axis=1))
        found.append(both[:size] + both[size:])
    return found


def forward(value, table_ref, rest):
    mixed = crossed(*[tile(value, s) for s in range(4)])
    high, low = split(tile(value, 4))
    both = jnp.where(lane_index() < 4 * rest, high.astype(f32), low.astype(f32)).astype(bf16)
    found = []
    for q in range(4):
        q_high, q_low = split(mixed[q])
        found.append(dot(jnp.concatenate([q_high, q_low, q_high, both, high], axis=1), table_ref[q]))
    return jnp.concatenate(
        [tile(v, 0) for v in found] + [tile(found[0], 1) + tile(found[1], 1), tile(found[2], 1) + tile(found[3], 1)],
        axis=1,
    )


def inverse_plane(modes, table_ref, rest):
    low_lanes = (lane_index() >= 2 * rest) & (lane_index() < 4 * rest)
    both = []
    for pair in range(2):
        value = tile(modes, 4 + pair)
        high = value.astype(bf16).astype(f32)
        both.append(jnp.where(low_lanes, value - high, high).astype(bf16))
    found = []
    for q in range(4):
        high, low = split(tile(modes, q))
        found.append(dot(jnp.concatenate([high, low, high, both[q // 2]], axis=1), table_ref[q]))
    main = crossed(*[tile(v, 0) for v in found])
    last = (tile(found[0], 1) + tile(found[1], 1)) + (tile(found[2], 1) + tile(found[3], 1))
    return jnp.concatenate(list(main) + [last], axis=1)


def collide(field_ref, modes_ref, sum_ref, kernel_ref, loss_ref, inverse_ref, forward_ref, rows_ref, count, rest, most):
    rows = field_ref.shape[0]
    cells = rows // count
    terms = kernel_ref.shape[0]
    together = max(n for n in range(1, most + 1) if terms % n == 0)
    main = 4 * lanes
    size = rows_ref.shape[2] // 2

    def scaled(factor):
        modes = modes_ref[...].reshape(cells, count, 6 * lanes)
        return (modes * factor[None]).reshape(rows, 6 * lanes)

    for k, part in enumerate(along_rows([forward(field_ref[...], forward_ref, rest)], rows_ref[0], size)):
        modes_ref[k * size : (k + 1) * size] = part
    plane = inverse_plane(scaled(loss_ref[...]), inverse_ref, rest)
    for k, part in enumerate(along_rows([plane], rows_ref[1], size)):
        at = slice(k * size, (k + 1) * size)
        sum_ref[at] = -field_ref[at] * part

    def term(step, carry):
        factors = [kernel_ref[together * step + k, side] for k in range(together) for side in range(2)]
        plane = inverse_plane(jnp.concatenate([scaled(f) for f in factors], axis=0), inverse_ref, rest)
        pairs = []
        for k in range(together):
            first, second = [plane[(2 * k + side) * rows : (2 * k + side + 1) * rows] for side in range(2)]
            shared = jnp.where(lane_index() < 4 * rest, tile(first, 4), tile(second, 4))
            pairs.append(jnp.concatenate([first[:, :main], second[:, :main], shared], axis=1))
        for k, part in enumerate(along_rows(pairs, rows_ref[1], size)):
            at = slice(k * size, (k + 1) * size)
            total = sum_ref[at, :main]
            last = sum_ref[at, main:]
            for pair in range(together):
                lane = pair * (2 * main + lanes)
                total = total + part[:, lane : lane + main] * part[:, lane + main : lane + 2 * main]
                shared = part[:, lane + 2 * main : lane + 2 * main + lanes]
                last = last + shared * pltpu.roll(shared, 4 * rest, 1)
            sum_ref[at, :main] = total
            sum_ref[at, main:] = last
        return carry

    lax.fori_loop(0, terms // together, term, 0)
    field_ref[...] = field_ref[...] + collide_step * sum_ref[...]


def one_hot(source_row, rows):
    index = lax.broadcasted_iota(jnp.int32, (rows, source_row.shape[1]), 0)
    return jnp.where(index == source_row, 1.0, 0.0).astype(bf16)


def moved(value, table):
    high, low = split(value)
    both = dot(jnp.concatenate([high, low], axis=0), table)
    return both[: value.shape[0]] + both[value.shape[0] :]


def moved_tiles(value, table):
    high, low = split(value)
    return dot(jnp.concatenate([high, low], axis=1), jnp.concatenate([table, table], axis=0))


def pack_kernel(count, source_ref, move_ref, a_ref, b_ref, loss_ref, out_ref, loss_out_ref, moves_ref, table_ref):
    @pl.when(pl.program_id(0) == 0)
    def _():
        table_ref[...] = one_hot(source_ref[...], count * count)

    for k in range(moves_ref.shape[0]):
        moves_ref[k] = one_hot(move_ref[k], 5 * lanes)

    def rows_of(ref):
        rows = ref.shape[0] // count
        return jnp.concatenate([ref[pl.ds(k, rows, stride=count), :] for k in range(count)], axis=1)

    terms = out_ref.shape[0]
    both = jnp.concatenate([rows_of(a_ref), rows_of(b_ref)], axis=0)
    both = moved(both, table_ref[...]).reshape(2, terms, count, 6 * lanes)
    for side in range(2):
        out_ref[:, side] = both[side]

    @pl.when(pl.program_id(0) == 0)
    def _():
        loss_out_ref[...] = moved(rows_of(loss_ref), table_ref[...])


class Cells:
    def __init__(self, cells_x, count, ys):
        plane = count * count
        self.count = count
        self.parts = [
            [(x, y) for x in range(cells_x) for y in ys if y * plane % lanes == shift] for shift in (0, lanes // 2)
        ]
        self.order = self.parts[0] + self.parts[1]
        self.size = len(self.order) * count

    def rows(self, x, y):
        at = self.order.index((x, y)) * self.count
        return slice(at, at + self.count)

    def part_rows(self, k):
        at = k * len(self.parts[0]) * self.count
        return slice(at, at + len(self.parts[k]) * self.count)


def two_rims(refs):
    return (refs[0].at[0], refs[0].at[1]) if len(refs) == 1 else refs


def first_kernel(
    count, rest, cells, cells_y,
    density_ref, below_ref, above_ref, kernel_ref, loss_ref, inverse_ref, forward_ref, rows_ref, speed_ref, moves_ref,
    field_ref, *refs,
):
    up_ref, down_ref = two_rims(refs[:-3])
    modes_ref, sum_ref, rim_ref = refs[-3:]
    cells_x = density_ref.shape[0]
    middle = count // 2
    plane = count * count
    for i in range(2):
        rim_ref[i, :middle] = above_ref[i]
        rim_ref[i, middle:] = below_ref[i]
    positive = lax.broadcasted_iota(jnp.int32, (count, 1), 0) >= middle

    def behind(x):
        return density_ref[x] if x >= 0 else rim_ref[x + 2]

    def ahead(x):
        return density_ref[x] if x < cells_x else rim_ref[x - cells_x]

    w0, w1, w2 = [speed_ref[:, k : k + 1] for k in range(3)]
    moved_on = []
    for x in range(cells_x):
        near = jnp.where(positive, behind(x - 1), ahead(x + 1))
        far = jnp.where(positive, behind(x - 2), ahead(x + 2))
        moved_on.append(w0 * density_ref[x] + w1 * near + w2 * far)
    for k, part in enumerate(cells.parts):
        starts = [(x, y * plane // lanes * lanes) for x, y in part]
        values = jnp.concatenate([moved_on[x][:, at : at + 5 * lanes] for x, at in starts], axis=0)
        field_ref[cells.part_rows(k)] = moved_tiles(values, moves_ref[k])
    collide(field_ref, modes_ref, sum_ref, kernel_ref, loss_ref, inverse_ref, forward_ref, rows_ref, count, rest, 2)
    for x in range(cells_x):
        for k in range(2):
            up_ref[x, k] = field_ref[cells.rows(x, cells_y - 2 + k), 2 * lanes :]
            down_ref[x, k, :, : 2 * lanes] = field_ref[cells.rows(x, k), : 2 * lanes]
            down_ref[x, k, :, 2 * lanes :] = field_ref[cells.rows(x, k), 4 * lanes :]


def sweep_y(given_ref, below_ref, above_ref, speed_ref, field_ref, everything, cells, cells_y, rest):
    backward_last = (lane_index() // (2 * rest)) % 2 == 1

    def cell(x, y, part):
        if y < 0:
            return below_ref[x, y + 2, :, (part - 2) * lanes : (part - 1) * lanes]
        if y >= cells_y:
            at = part if part < 2 else 2
            return above_ref[x, y - cells_y, :, at * lanes : (at + 1) * lanes]
        return given_ref[everything.rows(x, y), part * lanes : (part + 1) * lanes]

    for x, y in cells.order:
        for part in range(5):
            w0, w1, w2 = [speed_ref[k : k + 1, part * lanes : (part + 1) * lanes] for k in range(3)]
            if part < 2:
                near, far = cell(x, y + 1, part), cell(x, y + 2, part)
            elif part < 4:
                near, far = cell(x, y - 1, part), cell(x, y - 2, part)
            else:
                near = jnp.where(backward_last, cell(x, y - 1, part), cell(x, y + 1, part))
                far = jnp.where(backward_last, cell(x, y - 2, part), cell(x, y + 2, part))
            field_ref[cells.rows(x, y), part * lanes : (part + 1) * lanes] = (
                w0 * cell(x, y, part) + w1 * near + w2 * far
            )


def inner_kernel(
    count, rest, everything, cells, cells_y,
    given_ref, kernel_ref, loss_ref, inverse_ref, forward_ref, rows_ref, speed_ref,
    field_ref, modes_ref, sum_ref,
):
    sweep_y(given_ref, None, None, speed_ref, field_ref, everything, cells, cells_y, rest)
    collide(field_ref, modes_ref, sum_ref, kernel_ref, loss_ref, inverse_ref, forward_ref, rows_ref, count, rest, 4)


def outer_kernel(
    count, rest, everything, inner, cells, cells_y,
    given_ref, inner_ref, kernel_ref, loss_ref, inverse_ref, forward_ref, rows_ref, speed_ref, moves_ref, *refs,
):
    below_ref, above_ref = two_rims(refs[:-4])
    out_ref, field_ref, modes_ref, sum_ref = refs[-4:]
    plane = count * count
    sweep_y(given_ref, below_ref, above_ref, speed_ref, field_ref, everything, cells, cells_y, rest)
    collide(field_ref, modes_ref, sum_ref, kernel_ref, loss_ref, inverse_ref, forward_ref, rows_ref, count, rest, 2)
    pieces = {}
    for k in range(2):
        values = [field_ref[cells.part_rows(k)], inner_ref[inner.part_rows(k)]]
        natural = moved_tiles(jnp.concatenate(values, axis=0), moves_ref[2 + k])
        for i, place in enumerate(cells.parts[k] + inner.parts[k]):
            pieces[place] = natural[i * count : (i + 1) * count]
    for x in range(out_ref.shape[0]):
        filled = {}
        for y in range(cells_y):
            first = y * plane // lanes
            for t in range(5):
                value = tile(pieces[x, y], t)
                filled[first + t] = filled[first + t] + value if first + t in filled else value
        for t in range(out_ref.shape[2] // lanes):
            out_ref[x, :, t * lanes : (t + 1) * lanes] = filled[t]


def body(density, gains_a, gains_b, loss_rates):
    cells_x, count, width = density.shape
    terms = gains_a.shape[0]
    middle = count // 2
    plane = count * count
    cells_y = width // plane
    rest = middle * middle - lanes
    everything = Cells(cells_x, count, range(cells_y))
    inner = Cells(cells_x, count, range(2, cells_y - 2))
    outer = Cells(cells_x, count, [*range(2), *range(cells_y - 2, cells_y)])
    points = point_lanes(count)
    moves = np.full((4, 1, 5 * lanes), -1, np.int32)
    for k in range(2):
        shift = k * lanes // 2
        moves[k, 0] = np.where(points >= 0, points + shift, -1)
        for lane in range(4 * lanes + 4 * rest):
            moves[2 + k, 0, points[lane] + shift] = lane
    weights = courant_weights(count)
    lane_speed = np.where(points >= 0, weights[:, points // count], 0.0).astype(np.float32)
    lane_speed = jnp.asarray(lane_speed)
    row_speed = jnp.asarray(weights.T.astype(np.float32))
    group = min(cells_together(c.size // count) for c in (everything, inner, outer))
    tables = [jnp.asarray(t) for t in (inverse_tables(count), forward_tables(count), row_tables(count, group))]

    def params(mib):
        return pltpu.CompilerParams(vmem_limit_bytes=mib << 20)

    def scratch(cells):
        return [pltpu.VMEM((cells.size, k * lanes), f32) for k in (6, 5)]

    def cost(cells):
        return pl.CostEstimate(flops=cells.size << 27, bytes_accessed=4 << 20, transcendentals=0)

    below = passed_along(density[-2:, middle:], "gx", 1)
    above = passed_along(density[:2, :middle], "gx", -1)
    steps = 2 if terms % 2 == 0 else 1
    taken = terms // steps
    gain_spec = pl.BlockSpec((taken * plane, count), lambda i: (i, 0))
    packed, packed_loss, move_tables = pl.pallas_call(
        functools.partial(pack_kernel, count),
        grid=(steps,),
        in_specs=[
            pl.BlockSpec((1, 6 * lanes), lambda i: (0, 0)),
            pl.BlockSpec((4 // steps, 1, 5 * lanes), lambda i: (i, 0, 0)),
            gain_spec,
            gain_spec,
            pl.BlockSpec((plane, count), lambda i: (0, 0)),
        ],
        out_specs=[
            pl.BlockSpec((taken, 2, count, 6 * lanes), lambda i: (i, 0, 0, 0)),
            pl.BlockSpec((count, 6 * lanes), lambda i: (0, 0)),
            pl.BlockSpec((4 // steps, 5 * lanes, 5 * lanes), lambda i: (i, 0, 0)),
        ],
        out_shape=(
            jax.ShapeDtypeStruct((terms, 2, count, 6 * lanes), f32),
            jax.ShapeDtypeStruct((count, 6 * lanes), f32),
            jax.ShapeDtypeStruct((4, 5 * lanes, 5 * lanes), bf16),
        ),
        scratch_shapes=[pltpu.VMEM((plane, 6 * lanes), bf16)],
        compiler_params=params(pack_mib),
        cost_estimate=pl.CostEstimate(flops=4 << 30, bytes_accessed=8 << 20, transcendentals=0),
        name="pack",
    )(
        jnp.asarray(mode_lanes(count)[None]),
        jnp.asarray(moves),
        gains_a.reshape(-1, count),
        gains_b.reshape(-1, count),
        loss_rates.reshape(-1, count),
    )
    rim = (cells_x, 2, count, 3 * lanes)
    mirrored = lax.axis_size("gy") == 2
    rim_shapes = [jax.ShapeDtypeStruct((2, *rim), f32)] if mirrored else [jax.ShapeDtypeStruct(rim, f32)] * 2
    field, *rims = pl.pallas_call(
        functools.partial(first_kernel, count, rest, everything, cells_y),
        out_shape=(jax.ShapeDtypeStruct((everything.size, 5 * lanes), f32), *rim_shapes),
        scratch_shapes=scratch(everything) + [pltpu.VMEM((2, count, width), f32)],
        compiler_params=params(first_mib),
        cost_estimate=cost(everything),
        name="first",
    )(density, below, above, packed, packed_loss, *tables, row_speed, move_tables)
    rims = [passed_along(value, "gy", steps) for value, steps in zip(rims, (1, -1))]
    inner_field = pl.pallas_call(
        functools.partial(inner_kernel, count, rest, everything, inner, cells_y),
        out_shape=jax.ShapeDtypeStruct((inner.size, 5 * lanes), f32),
        scratch_shapes=scratch(inner),
        compiler_params=params(second_mib),
        cost_estimate=cost(inner),
        name="inner",
    )(field, packed, packed_loss, *tables, lane_speed)
    return pl.pallas_call(
        functools.partial(outer_kernel, count, rest, everything, inner, outer, cells_y),
        out_shape=jax.ShapeDtypeStruct(density.shape, f32),
        scratch_shapes=[pltpu.VMEM((outer.size, 5 * lanes), f32)] + scratch(outer),
        compiler_params=params(second_mib),
        cost_estimate=cost(outer),
        name="outer",
    )(field, inner_field, packed, packed_loss, *tables, lane_speed, move_tables, *rims)


def solution(mesh):
    in_specs = (P("gx", None, "gy"), P(), P(), P())
    out_specs = P("gx", None, "gy")
    return jax.shard_map(body, mesh=mesh, in_specs=in_specs, out_specs=out_specs, check_vma=False)
```

```python
import functools

import jax
import jax.numpy as jnp
import numpy as np
from jax import lax
from jax.experimental import pallas as pl
from jax.experimental.pallas import tpu as pltpu
from jax.sharding import PartitionSpec as P

courant_max = 1.6
collide_step = 0.2
lanes = 128
pack_mib, first_mib, second_mib = 24, 28, 24
bf16 = jnp.bfloat16
f32 = jnp.float32
dot = functools.partial(jnp.dot, preferred_element_type=f32)


def passed_along(value, axis, steps):
    count = lax.axis_size(axis)
    pairs = [(source, (source + steps) % count) for source in range(count)]
    return lax.ppermute(value, axis, pairs)


def passed_along_line(value, axis, steps):
    count = lax.axis_size(axis)
    return lax.ppermute(value, axis, [(k, k + steps) for k in range(count) if 0 <= k + steps < count])


def cosine_table(count):
    freq = np.arange(count)[:, None]
    points = np.arange(count)[None, :]
    scale = np.where(freq == 0, np.sqrt(1.0 / count), np.sqrt(2.0 / count))
    return scale * np.cos(np.pi * (2.0 * points + 1.0) * freq / (2.0 * count))


def two_parts(table):
    high = np.asarray(table, np.float32).astype(bf16)
    return high, (table - high.astype(np.float64)).astype(np.float32).astype(bf16)


def courant_weights(count):
    speeds = np.arange(count) - (count - 1) / 2.0
    a = courant_max * np.abs(speeds) / ((count - 1) / 2.0)
    return np.stack([1.0 - 1.5 * a + 0.5 * a * a, 2.0 * a - a * a, 0.5 * (a * a - a)])


def sign(s, q):
    return -1.0 if ((s >> 1) & (q >> 1)) ^ (s & 1 & q) else 1.0


def block_table(count, q):
    c = cosine_table(count)
    half = count // 2
    return np.kron(c[q >> 1 :: 2, :half], c[q & 1 :: 2, :half])


def point_lanes(count):
    half = count // 2
    block = half * half
    rest = block - lanes
    source = np.full(5 * lanes, -1, np.int32)
    for s in range(4):
        for m in range(block):
            j, l = divmod(m, half)
            y = count - 1 - j if s >> 1 else j
            z = count - 1 - l if s & 1 else l
            if m < lanes:
                source[s * lanes + m] = y * count + z
            else:
                for copy in range(2):
                    source[4 * lanes + copy * 4 * rest + s * rest + m - lanes] = y * count + z
    return source


def mode_lanes(count):
    half = count // 2
    block = half * half
    rest = block - lanes
    source = np.full(6 * lanes, -1, np.int32)
    for q in range(4):
        for m in range(block):
            j, l = divmod(m, half)
            place = (2 * j + (q >> 1)) * count + 2 * l + (q & 1)
            if m < lanes:
                source[q * lanes + m] = place
            else:
                for copy in range(3):
                    source[(4 + q // 2) * lanes + copy * 2 * rest + (q % 2) * rest + m - lanes] = place
    return source


def inverse_tables(count):
    rest = (count // 2) ** 2 - lanes
    out = np.zeros((4, 4 * lanes, 2 * lanes), bf16)
    for q in range(4):
        table = block_table(count, q)
        wide = np.zeros((table.shape[0], 2 * lanes))
        wide[:, :lanes] = table[:, :lanes]
        for s in range(4):
            for copy in range(2):
                at = lanes + copy * 4 * rest + s * rest
                wide[:, at : at + rest] = sign(s, q) * table[:, lanes:]
        high, low = two_parts(wide)
        out[q, :lanes] = high[:lanes]
        out[q, lanes : 2 * lanes] = high[:lanes]
        out[q, 2 * lanes : 3 * lanes] = low[:lanes]
        for copy, part in enumerate((high, high, low)):
            at = 3 * lanes + copy * 2 * rest + (q % 2) * rest
            out[q, at : at + rest] = part[lanes:]
    return out


def forward_tables(count):
    rest = (count // 2) ** 2 - lanes
    out = np.zeros((4, 5 * lanes, 2 * lanes), bf16)
    for q in range(4):
        table = block_table(count, q).T
        wide = np.zeros((table.shape[0], 2 * lanes))
        wide[:, :lanes] = table[:, :lanes]
        for copy in range(3):
            at = lanes + copy * 2 * rest + (q % 2) * rest
            wide[:, at : at + rest] = table[:, lanes:]
        high, low = two_parts(wide)
        out[q, :lanes] = high[:lanes]
        out[q, lanes : 2 * lanes] = high[:lanes]
        out[q, 2 * lanes : 3 * lanes] = low[:lanes]
        for s in range(4):
            for at, part in ((3 * lanes, high), (3 * lanes + 4 * rest, high), (4 * lanes, low)):
                at = at + s * rest
                out[q, at : at + rest] = (sign(s, q) * part[lanes:].astype(np.float32)).astype(bf16)
    return out


def cells_together(cells):
    return max(n for n in (1, 2, 4) if cells % n == 0)


def row_tables(count, cells):
    c = cosine_table(count)
    result = []
    for table in (c, c.T):
        coarse, fine = two_parts(np.kron(np.eye(cells), table))
        upper = np.concatenate([coarse, coarse], axis=1)
        lower = np.concatenate([fine, np.zeros_like(fine)], axis=1)
        result.append(np.concatenate([upper, lower], axis=0))
    return np.stack(result)


def split(value):
    high = value.astype(bf16)
    return high, (value - high.astype(f32)).astype(bf16)


def lane_index():
    return lax.broadcasted_iota(jnp.int32, (1, lanes), 1)


def tile(value, at):
    return value[:, at * lanes : (at + 1) * lanes]


def crossed(v0, v1, v2, v3):
    t0, t1, t2, t3 = v0 + v1, v0 - v1, v2 + v3, v2 - v3
    return t0 + t2, t1 + t3, t0 - t2, t1 - t3


def along_rows(values, table, size):
    parts = [split(value) for value in values]
    found = []
    for at in range(0, values[0].shape[0], size):
        pieces = [jnp.concatenate([high[at : at + size], low[at : at + size]], axis=0) for high, low in parts]
        both = dot(table, jnp.concatenate(pieces, axis=1))
        found.append(both[:size] + both[size:])
    return found


def forward(value, table_ref, rest):
    mixed = crossed(*[tile(value, s) for s in range(4)])
    high, low = split(tile(value, 4))
    both = jnp.where(lane_index() < 4 * rest, high.astype(f32), low.astype(f32)).astype(bf16)
    found = []
    for q in range(4):
        q_high, q_low = split(mixed[q])
        found.append(dot(jnp.concatenate([q_high, q_low, q_high, both, high], axis=1), table_ref[q]))
    return jnp.concatenate(
        [tile(v, 0) for v in found] + [tile(found[0], 1) + tile(found[1], 1), tile(found[2], 1) + tile(found[3], 1)],
        axis=1,
    )


def inverse_plane(modes, table_ref, rest):
    low_lanes = (lane_index() >= 2 * rest) & (lane_index() < 4 * rest)
    both = []
    for pair in range(2):
        value = tile(modes, 4 + pair)
        high = value.astype(bf16).astype(f32)
        both.append(jnp.where(low_lanes, value - high, high).astype(bf16))
    found = []
    for q in range(4):
        high, low = split(tile(modes, q))
        found.append(dot(jnp.concatenate([high, low, high, both[q // 2]], axis=1), table_ref[q]))
    main = crossed(*[tile(v, 0) for v in found])
    last = (tile(found[0], 1) + tile(found[1], 1)) + (tile(found[2], 1) + tile(found[3], 1))
    return jnp.concatenate(list(main) + [last], axis=1)


def collide(field_ref, modes_ref, sum_ref, kernel_ref, loss_ref, inverse_ref, forward_ref, rows_ref, count, rest, most):
    rows = field_ref.shape[0]
    cells = rows // count
    terms = kernel_ref.shape[0]
    together = max(n for n in range(1, most + 1) if terms % n == 0)
    main = 4 * lanes
    size = rows_ref.shape[2] // 2

    def scaled(factor):
        modes = modes_ref[...].reshape(cells, count, 6 * lanes)
        return (modes * factor[None]).reshape(rows, 6 * lanes)

    for k, part in enumerate(along_rows([forward(field_ref[...], forward_ref, rest)], rows_ref[0], size)):
        modes_ref[k * size : (k + 1) * size] = part
    plane = inverse_plane(scaled(loss_ref[...]), inverse_ref, rest)
    for k, part in enumerate(along_rows([plane], rows_ref[1], size)):
        at = slice(k * size, (k + 1) * size)
        sum_ref[at] = -field_ref[at] * part

    def term(step, carry):
        factors = [kernel_ref[together * step + k, side] for k in range(together) for side in range(2)]
        plane = inverse_plane(jnp.concatenate([scaled(f) for f in factors], axis=0), inverse_ref, rest)
        pairs = []
        for k in range(together):
            first, second = [plane[(2 * k + side) * rows : (2 * k + side + 1) * rows] for side in range(2)]
            shared = jnp.where(lane_index() < 4 * rest, tile(first, 4), tile(second, 4))
            pairs.append(jnp.concatenate([first[:, :main], second[:, :main], shared], axis=1))
        for k, part in enumerate(along_rows(pairs, rows_ref[1], size)):
            at = slice(k * size, (k + 1) * size)
            total = sum_ref[at, :main]
            last = sum_ref[at, main:]
            for pair in range(together):
                lane = pair * (2 * main + lanes)
                total = total + part[:, lane : lane + main] * part[:, lane + main : lane + 2 * main]
                shared = part[:, lane + 2 * main : lane + 2 * main + lanes]
                last = last + shared * pltpu.roll(shared, 4 * rest, 1)
            sum_ref[at, :main] = total
            sum_ref[at, main:] = last
        return carry

    lax.fori_loop(0, terms // together, term, 0)
    field_ref[...] = field_ref[...] + collide_step * sum_ref[...]


def one_hot(source_row, rows):
    index = lax.broadcasted_iota(jnp.int32, (rows, source_row.shape[1]), 0)
    return jnp.where(index == source_row, 1.0, 0.0).astype(bf16)


def moved(value, table):
    high, low = split(value)
    both = dot(jnp.concatenate([high, low], axis=0), table)
    return both[: value.shape[0]] + both[value.shape[0] :]


def moved_tiles(value, table):
    high, low = split(value)
    return dot(jnp.concatenate([high, low], axis=1), jnp.concatenate([table, table], axis=0))


def pack_kernel(count, source_ref, move_ref, a_ref, b_ref, loss_ref, out_ref, loss_out_ref, moves_ref, table_ref):
    @pl.when(pl.program_id(0) == 0)
    def _():
        table_ref[...] = one_hot(source_ref[...], count * count)

    for k in range(moves_ref.shape[0]):
        moves_ref[k] = one_hot(move_ref[k], 5 * lanes)

    def rows_of(ref):
        rows = ref.shape[0] // count
        return jnp.concatenate([ref[pl.ds(k, rows, stride=count), :] for k in range(count)], axis=1)

    terms = out_ref.shape[0]
    both = jnp.concatenate([rows_of(a_ref), rows_of(b_ref)], axis=0)
    both = moved(both, table_ref[...]).reshape(2, terms, count, 6 * lanes)
    for side in range(2):
        out_ref[:, side] = both[side]

    @pl.when(pl.program_id(0) == 0)
    def _():
        loss_out_ref[...] = moved(rows_of(loss_ref), table_ref[...])


class Cells:
    def __init__(self, cells_x, count, ys):
        plane = count * count
        self.count = count
        self.parts = [
            [(x, y) for x in range(cells_x) for y in ys if y * plane % lanes == shift] for shift in (0, lanes // 2)
        ]
        self.order = self.parts[0] + self.parts[1]
        self.size = len(self.order) * count

    def rows(self, x, y):
        at = self.order.index((x, y)) * self.count
        return slice(at, at + self.count)

    def part_rows(self, k):
        at = k * len(self.parts[0]) * self.count
        return slice(at, at + len(self.parts[k]) * self.count)


def two_rims(refs):
    return (refs[0].at[0], refs[0].at[1]) if len(refs) == 1 else refs


def first_kernel(
    count, rest, cells, cells_y,
    density_ref, below_ref, above_ref, closing_ref, is_end_ref,
    kernel_ref, loss_ref, inverse_ref, forward_ref, rows_ref, speed_ref, moves_ref,
    field_ref, *refs,
):
    up_ref, down_ref = two_rims(refs[:-3])
    modes_ref, sum_ref, rim_ref = refs[-3:]
    cells_x = density_ref.shape[0]
    middle = count // 2
    plane = count * count
    for i in range(2):
        rim_ref[i, :middle] = above_ref[i]
        rim_ref[i, middle:] = below_ref[i]

    @pl.when(is_end_ref[0] == 1)
    def _():
        for i in range(2):
            rim_ref[i, :middle] = closing_ref[i]

    @pl.when(is_end_ref[1] == 1)
    def _():
        for i in range(2):
            rim_ref[i, middle:] = closing_ref[i]

    positive = lax.broadcasted_iota(jnp.int32, (count, 1), 0) >= middle

    def behind(x):
        return density_ref[x] if x >= 0 else rim_ref[x + 2]

    def ahead(x):
        return density_ref[x] if x < cells_x else rim_ref[x - cells_x]

    w0, w1, w2 = [speed_ref[:, k : k + 1] for k in range(3)]
    moved_on = []
    for x in range(cells_x):
        near = jnp.where(positive, behind(x - 1), ahead(x + 1))
        far = jnp.where(positive, behind(x - 2), ahead(x + 2))
        moved_on.append(w0 * density_ref[x] + w1 * near + w2 * far)
    for k, part in enumerate(cells.parts):
        starts = [(x, y * plane // lanes * lanes) for x, y in part]
        values = jnp.concatenate([moved_on[x][:, at : at + 5 * lanes] for x, at in starts], axis=0)
        field_ref[cells.part_rows(k)] = moved_tiles(values, moves_ref[k])
    collide(field_ref, modes_ref, sum_ref, kernel_ref, loss_ref, inverse_ref, forward_ref, rows_ref, count, rest, 2)
    for x in range(cells_x):
        for k in range(2):
            up_ref[x, k] = field_ref[cells.rows(x, cells_y - 2 + k), 2 * lanes :]
            down_ref[x, k, :, : 2 * lanes] = field_ref[cells.rows(x, k), : 2 * lanes]
            down_ref[x, k, :, 2 * lanes :] = field_ref[cells.rows(x, k), 4 * lanes :]


def sweep_y(given_ref, below_ref, above_ref, speed_ref, field_ref, everything, cells, cells_y, rest):
    backward_last = (lane_index() // (2 * rest)) % 2 == 1

    def cell(x, y, part):
        if y < 0:
            return below_ref[x, y + 2, :, (part - 2) * lanes : (part - 1) * lanes]
        if y >= cells_y:
            at = part if part < 2 else 2
            return above_ref[x, y - cells_y, :, at * lanes : (at + 1) * lanes]
        return given_ref[everything.rows(x, y), part * lanes : (part + 1) * lanes]

    for x, y in cells.order:
        for part in range(5):
            w0, w1, w2 = [speed_ref[k : k + 1, part * lanes : (part + 1) * lanes] for k in range(3)]
            if part < 2:
                near, far = cell(x, y + 1, part), cell(x, y + 2, part)
            elif part < 4:
                near, far = cell(x, y - 1, part), cell(x, y - 2, part)
            else:
                near = jnp.where(backward_last, cell(x, y - 1, part), cell(x, y + 1, part))
                far = jnp.where(backward_last, cell(x, y - 2, part), cell(x, y + 2, part))
            field_ref[cells.rows(x, y), part * lanes : (part + 1) * lanes] = (
                w0 * cell(x, y, part) + w1 * near + w2 * far
            )


def inner_kernel(
    count, rest, everything, cells, cells_y,
    given_ref, kernel_ref, loss_ref, inverse_ref, forward_ref, rows_ref, speed_ref,
    field_ref, modes_ref, sum_ref,
):
    sweep_y(given_ref, None, None, speed_ref, field_ref, everything, cells, cells_y, rest)
    collide(field_ref, modes_ref, sum_ref, kernel_ref, loss_ref, inverse_ref, forward_ref, rows_ref, count, rest, 4)


def outer_kernel(
    count, rest, everything, inner, cells, cells_y,
    given_ref, inner_ref, kernel_ref, loss_ref, inverse_ref, forward_ref, rows_ref, speed_ref, moves_ref, *refs,
):
    below_ref, above_ref = two_rims(refs[:-4])
    out_ref, field_ref, modes_ref, sum_ref = refs[-4:]
    plane = count * count
    sweep_y(given_ref, below_ref, above_ref, speed_ref, field_ref, everything, cells, cells_y, rest)
    collide(field_ref, modes_ref, sum_ref, kernel_ref, loss_ref, inverse_ref, forward_ref, rows_ref, count, rest, 2)
    pieces = {}
    for k in range(2):
        values = [field_ref[cells.part_rows(k)], inner_ref[inner.part_rows(k)]]
        natural = moved_tiles(jnp.concatenate(values, axis=0), moves_ref[2 + k])
        for i, place in enumerate(cells.parts[k] + inner.parts[k]):
            pieces[place] = natural[i * count : (i + 1) * count]
    for x in range(out_ref.shape[0]):
        filled = {}
        for y in range(cells_y):
            first = y * plane // lanes
            for t in range(5):
                value = tile(pieces[x, y], t)
                filled[first + t] = filled[first + t] + value if first + t in filled else value
        for t in range(out_ref.shape[2] // lanes):
            out_ref[x, :, t * lanes : (t + 1) * lanes] = filled[t]


def body(density, gains_a, gains_b, loss_rates):
    cells_x, count, width = density.shape
    terms = gains_a.shape[0]
    middle = count // 2
    plane = count * count
    cells_y = width // plane
    rest = middle * middle - lanes
    everything = Cells(cells_x, count, range(cells_y))
    inner = Cells(cells_x, count, range(2, cells_y - 2))
    outer = Cells(cells_x, count, [*range(2), *range(cells_y - 2, cells_y)])
    points = point_lanes(count)
    moves = np.full((4, 1, 5 * lanes), -1, np.int32)
    for k in range(2):
        shift = k * lanes // 2
        moves[k, 0] = np.where(points >= 0, points + shift, -1)
        for lane in range(4 * lanes + 4 * rest):
            moves[2 + k, 0, points[lane] + shift] = lane
    weights = courant_weights(count)
    lane_speed = np.where(points >= 0, weights[:, points // count], 0.0).astype(np.float32)
    lane_speed = jnp.asarray(lane_speed)
    row_speed = jnp.asarray(weights.T.astype(np.float32))
    group = min(cells_together(c.size // count) for c in (everything, inner, outer))
    tables = [jnp.asarray(t) for t in (inverse_tables(count), forward_tables(count), row_tables(count, group))]

    whole = pl.BlockSpec(memory_space=pltpu.VMEM)

    def params(mib):
        return pltpu.CompilerParams(vmem_limit_bytes=mib << 20)

    def scratch(cells):
        return [pltpu.VMEM((cells.size, k * lanes), f32) for k in (6, 5)]

    def cost(cells):
        return pl.CostEstimate(flops=cells.size << 27, bytes_accessed=4 << 20, transcendentals=0)

    place = lax.axis_index("gx")
    ends = lax.axis_size("gx")
    leaving_up, leaving_down = density[-2:, middle:], density[:2, :middle]
    closing = lax.ppermute(
        jnp.where(place == 0, leaving_down, leaving_up), "gx", [(0, ends - 1), (ends - 1, 0)]
    )
    below = passed_along_line(leaving_up, "gx", 1)
    above = passed_along_line(leaving_down, "gx", -1)
    is_end = jnp.stack([place == ends - 1, place == 0]).astype(jnp.int32)
    steps = 2 if terms % 2 == 0 else 1
    taken = terms // steps
    gain_spec = pl.BlockSpec((taken * plane, count), lambda i: (i, 0))
    packed, packed_loss, move_tables = pl.pallas_call(
        functools.partial(pack_kernel, count),
        grid=(steps,),
        in_specs=[
            pl.BlockSpec((1, 6 * lanes), lambda i: (0, 0)),
            pl.BlockSpec((4 // steps, 1, 5 * lanes), lambda i: (i, 0, 0)),
            gain_spec,
            gain_spec,
            pl.BlockSpec((plane, count), lambda i: (0, 0)),
        ],
        out_specs=[
            pl.BlockSpec((taken, 2, count, 6 * lanes), lambda i: (i, 0, 0, 0)),
            pl.BlockSpec((count, 6 * lanes), lambda i: (0, 0)),
            pl.BlockSpec((4 // steps, 5 * lanes, 5 * lanes), lambda i: (i, 0, 0)),
        ],
        out_shape=(
            jax.ShapeDtypeStruct((terms, 2, count, 6 * lanes), f32),
            jax.ShapeDtypeStruct((count, 6 * lanes), f32),
            jax.ShapeDtypeStruct((4, 5 * lanes, 5 * lanes), bf16),
        ),
        scratch_shapes=[pltpu.VMEM((plane, 6 * lanes), bf16)],
        compiler_params=params(pack_mib),
        cost_estimate=pl.CostEstimate(flops=4 << 30, bytes_accessed=8 << 20, transcendentals=0),
        name="pack",
    )(
        jnp.asarray(mode_lanes(count)[None]),
        jnp.asarray(moves),
        pltpu.with_memory_space_constraint(gains_a.reshape(-1, count), pltpu.HBM),
        pltpu.with_memory_space_constraint(gains_b.reshape(-1, count), pltpu.HBM),
        pltpu.with_memory_space_constraint(loss_rates.reshape(-1, count), pltpu.HBM),
    )
    rim = (cells_x, 2, count, 3 * lanes)
    mirrored = lax.axis_size("gy") == 2
    rim_shapes = [jax.ShapeDtypeStruct((2, *rim), f32)] if mirrored else [jax.ShapeDtypeStruct(rim, f32)] * 2
    field, *rims = pl.pallas_call(
        functools.partial(first_kernel, count, rest, everything, cells_y),
        in_specs=[whole] * 4 + [pl.BlockSpec(memory_space=pltpu.SMEM)] + [whole] * 7,
        out_shape=(jax.ShapeDtypeStruct((everything.size, 5 * lanes), f32), *rim_shapes),
        scratch_shapes=scratch(everything) + [pltpu.VMEM((2, count, width), f32)],
        compiler_params=params(first_mib),
        cost_estimate=cost(everything),
        name="first",
    )(density, below, above, closing, is_end, packed, packed_loss, *tables, row_speed, move_tables)
    rims = [passed_along(value, "gy", steps) for value, steps in zip(rims, (1, -1))]
    inner_field = pl.pallas_call(
        functools.partial(inner_kernel, count, rest, everything, inner, cells_y),
        out_shape=jax.ShapeDtypeStruct((inner.size, 5 * lanes), f32),
        scratch_shapes=scratch(inner),
        compiler_params=params(second_mib),
        cost_estimate=cost(inner),
        name="inner",
    )(field, packed, packed_loss, *tables, lane_speed)
    return pl.pallas_call(
        functools.partial(outer_kernel, count, rest, everything, inner, outer, cells_y),
        out_shape=jax.ShapeDtypeStruct(density.shape, f32),
        scratch_shapes=[pltpu.VMEM((outer.size, 5 * lanes), f32)] + scratch(outer),
        compiler_params=params(second_mib),
        cost_estimate=cost(outer),
        name="outer",
    )(field, inner_field, packed, packed_loss, *tables, lane_speed, move_tables, *rims)


def solution(mesh):
    in_specs = (P("gx", None, "gy"), P(), P(), P())
    out_specs = P("gx", None, "gy")
    return jax.shard_map(body, mesh=mesh, in_specs=in_specs, out_specs=out_specs, check_vma=False)
```

```python
import functools

import jax
import jax.numpy as jnp
import numpy as np
from jax import lax
from jax.experimental import pallas as pl
from jax.experimental.pallas import tpu as pltpu
from jax.sharding import PartitionSpec as P


courant_max = 1.6
collide_step = 0.2
lanes = 128
pack_mib, first_mib, second_mib = 24, 28, 24
bf16 = jnp.bfloat16
f32 = jnp.float32
dot = functools.partial(jnp.dot, preferred_element_type=f32)


def passed_along(value, axis, steps):
    count = lax.axis_size(axis)
    pairs = [(source, (source + steps) % count) for source in range(count)]
    return lax.ppermute(value, axis, pairs)


def cosine_table(count):
    freq = np.arange(count)[:, None]
    points = np.arange(count)[None, :]
    scale = np.where(freq == 0, np.sqrt(1.0 / count), np.sqrt(2.0 / count))
    return scale * np.cos(np.pi * (2.0 * points + 1.0) * freq / (2.0 * count))


def two_parts(table):
    high = np.asarray(table, np.float32).astype(bf16)
    return high, (table - high.astype(np.float64)).astype(np.float32).astype(bf16)


def courant_weights(count):
    speeds = np.arange(count) - (count - 1) / 2.0
    a = courant_max * np.abs(speeds) / ((count - 1) / 2.0)
    return np.stack([1.0 - 1.5 * a + 0.5 * a * a, 2.0 * a - a * a, 0.5 * (a * a - a)])


def sign(s, q):
    return -1.0 if ((s >> 1) & (q >> 1)) ^ (s & 1 & q) else 1.0


def block_table(count, q):
    c = cosine_table(count)
    half = count // 2
    return np.kron(c[q >> 1 :: 2, :half], c[q & 1 :: 2, :half])


def point_lanes(count):
    half = count // 2
    block = half * half
    rest = block - lanes
    source = np.full(5 * lanes, -1, np.int32)
    for s in range(4):
        for m in range(block):
            j, l = divmod(m, half)
            y = count - 1 - j if s >> 1 else j
            z = count - 1 - l if s & 1 else l
            if m < lanes:
                source[s * lanes + m] = y * count + z
            else:
                for copy in range(2):
                    source[4 * lanes + copy * 4 * rest + s * rest + m - lanes] = y * count + z
    return source


def mode_lanes(count):
    half = count // 2
    block = half * half
    rest = block - lanes
    source = np.full(6 * lanes, -1, np.int32)
    for q in range(4):
        for m in range(block):
            j, l = divmod(m, half)
            place = (2 * j + (q >> 1)) * count + 2 * l + (q & 1)
            if m < lanes:
                source[q * lanes + m] = place
            else:
                for copy in range(3):
                    source[(4 + q // 2) * lanes + copy * 2 * rest + (q % 2) * rest + m - lanes] = place
    return source


def inverse_tables(count):
    rest = (count // 2) ** 2 - lanes
    out = np.zeros((4, 4 * lanes, 2 * lanes), bf16)
    for q in range(4):
        table = block_table(count, q)
        wide = np.zeros((table.shape[0], 2 * lanes))
        wide[:, :lanes] = table[:, :lanes]
        for s in range(4):
            for copy in range(2):
                at = lanes + copy * 4 * rest + s * rest
                wide[:, at : at + rest] = sign(s, q) * table[:, lanes:]
        high, low = two_parts(wide)
        out[q, :lanes] = high[:lanes]
        out[q, lanes : 2 * lanes] = high[:lanes]
        out[q, 2 * lanes : 3 * lanes] = low[:lanes]
        for copy, part in enumerate((high, high, low)):
            at = 3 * lanes + copy * 2 * rest + (q % 2) * rest
            out[q, at : at + rest] = part[lanes:]
    return out


def forward_tables(count):
    rest = (count // 2) ** 2 - lanes
    out = np.zeros((4, 5 * lanes, 2 * lanes), bf16)
    for q in range(4):
        table = block_table(count, q).T
        wide = np.zeros((table.shape[0], 2 * lanes))
        wide[:, :lanes] = table[:, :lanes]
        for copy in range(3):
            at = lanes + copy * 2 * rest + (q % 2) * rest
            wide[:, at : at + rest] = table[:, lanes:]
        high, low = two_parts(wide)
        out[q, :lanes] = high[:lanes]
        out[q, lanes : 2 * lanes] = high[:lanes]
        out[q, 2 * lanes : 3 * lanes] = low[:lanes]
        for s in range(4):
            for at, part in ((3 * lanes, high), (3 * lanes + 4 * rest, high), (4 * lanes, low)):
                at = at + s * rest
                out[q, at : at + rest] = (sign(s, q) * part[lanes:].astype(np.float32)).astype(bf16)
    return out


def cells_together(cells):
    return max(n for n in (1, 2, 4) if cells % n == 0)


def row_tables(count, cells):
    c = cosine_table(count)
    result = []
    for table in (c, c.T):
        coarse, fine = two_parts(np.kron(np.eye(cells), table))
        upper = np.concatenate([coarse, coarse], axis=1)
        lower = np.concatenate([fine, np.zeros_like(fine)], axis=1)
        result.append(np.concatenate([upper, lower], axis=0))
    return np.stack(result)


def split(value):
    high = value.astype(bf16)
    return high, (value - high.astype(f32)).astype(bf16)


def lane_index():
    return lax.broadcasted_iota(jnp.int32, (1, lanes), 1)


def tile(value, at):
    return value[:, at * lanes : (at + 1) * lanes]


def crossed(v0, v1, v2, v3):
    t0, t1, t2, t3 = v0 + v1, v0 - v1, v2 + v3, v2 - v3
    return t0 + t2, t1 + t3, t0 - t2, t1 - t3


def along_rows(values, table, size):
    parts = [split(value) for value in values]
    found = []
    for at in range(0, values[0].shape[0], size):
        pieces = [jnp.concatenate([high[at : at + size], low[at : at + size]], axis=0) for high, low in parts]
        both = dot(table, jnp.concatenate(pieces, axis=1))
        found.append(both[:size] + both[size:])
    return found


def forward(value, table_ref, rest):
    mixed = crossed(*[tile(value, s) for s in range(4)])
    high, low = split(tile(value, 4))
    both = jnp.where(lane_index() < 4 * rest, high.astype(f32), low.astype(f32)).astype(bf16)
    found = []
    for q in range(4):
        q_high, q_low = split(mixed[q])
        found.append(dot(jnp.concatenate([q_high, q_low, q_high, both, high], axis=1), table_ref[q]))
    return jnp.concatenate(
        [tile(v, 0) for v in found] + [tile(found[0], 1) + tile(found[1], 1), tile(found[2], 1) + tile(found[3], 1)],
        axis=1,
    )


def inverse_plane(modes, table_ref, rest):
    low_lanes = (lane_index() >= 2 * rest) & (lane_index() < 4 * rest)
    both = []
    for pair in range(2):
        value = tile(modes, 4 + pair)
        high = value.astype(bf16).astype(f32)
        both.append(jnp.where(low_lanes, value - high, high).astype(bf16))
    found = []
    for q in range(4):
        high, low = split(tile(modes, q))
        found.append(dot(jnp.concatenate([high, low, high, both[q // 2]], axis=1), table_ref[q]))
    main = crossed(*[tile(v, 0) for v in found])
    last = (tile(found[0], 1) + tile(found[1], 1)) + (tile(found[2], 1) + tile(found[3], 1))
    return jnp.concatenate(list(main) + [last], axis=1)


def collide(field_ref, modes_ref, sum_ref, a_ref, b_ref, loss_ref, inverse_ref, forward_ref, rows_ref, count, rest, most):
    rows = field_ref.shape[0]
    cells = rows // count
    terms = a_ref.shape[0]
    together = max(n for n in range(1, most + 1) if terms % n == 0)
    main = 4 * lanes
    size = rows_ref.shape[2] // 2

    def scaled(factor):
        modes = modes_ref[...].reshape(cells, count, 6 * lanes)
        return (modes * factor[None]).reshape(rows, 6 * lanes)

    for k, part in enumerate(along_rows([forward(field_ref[...], forward_ref, rest)], rows_ref[0], size)):
        modes_ref[k * size : (k + 1) * size] = part
    plane = inverse_plane(scaled(loss_ref[...]), inverse_ref, rest)
    for k, part in enumerate(along_rows([plane], rows_ref[1], size)):
        at = slice(k * size, (k + 1) * size)
        sum_ref[at] = -field_ref[at] * part

    def term(step, carry):
        factors = [ref[together * step + k] for k in range(together) for ref in (a_ref, b_ref)]
        plane = inverse_plane(jnp.concatenate([scaled(f) for f in factors], axis=0), inverse_ref, rest)
        pairs = []
        for k in range(together):
            first, second = [plane[(2 * k + side) * rows : (2 * k + side + 1) * rows] for side in range(2)]
            shared = jnp.where(lane_index() < 4 * rest, tile(first, 4), tile(second, 4))
            pairs.append(jnp.concatenate([first[:, :main], second[:, :main], shared], axis=1))
        for k, part in enumerate(along_rows(pairs, rows_ref[1], size)):
            at = slice(k * size, (k + 1) * size)
            total = sum_ref[at, :main]
            last = sum_ref[at, main:]
            for pair in range(together):
                lane = pair * (2 * main + lanes)
                total = total + part[:, lane : lane + main] * part[:, lane + main : lane + 2 * main]
                shared = part[:, lane + 2 * main : lane + 2 * main + lanes]
                last = last + shared * pltpu.roll(shared, 4 * rest, 1)
            sum_ref[at, :main] = total
            sum_ref[at, main:] = last
        return carry

    lax.fori_loop(0, terms // together, term, 0)
    field_ref[...] = field_ref[...] + collide_step * sum_ref[...]


def one_hot(source_row, rows):
    index = lax.broadcasted_iota(jnp.int32, (rows, source_row.shape[1]), 0)
    return jnp.where(index == source_row, 1.0, 0.0).astype(bf16)


def moved(value, table):
    high, low = split(value)
    both = dot(jnp.concatenate([high, low], axis=0), table)
    return both[: value.shape[0]] + both[value.shape[0] :]


def moved_tiles(value, table):
    high, low = split(value)
    return dot(jnp.concatenate([high, low], axis=1), jnp.concatenate([table, table], axis=0))


def pack_kernel(count, source_ref, gain_ref, extra_ref, out_ref, extra_out_ref, table_ref):
    first = pl.program_id(0) == 0

    @pl.when(first)
    def _():
        table_ref[...] = one_hot(source_ref[...], count * count)

    def rows_of(ref):
        rows = ref.shape[0] // count
        return jnp.concatenate([ref[pl.ds(k, rows, stride=count), :] for k in range(count)], axis=1)

    out_ref[...] = moved(rows_of(gain_ref), table_ref[...]).reshape(out_ref.shape)
    if extra_ref.shape[1] == count:

        @pl.when(first)
        def _():
            extra_out_ref[...] = moved(rows_of(extra_ref), table_ref[...])

    else:
        for k in range(extra_ref.shape[0]):
            extra_out_ref[k] = one_hot(extra_ref[k], 5 * lanes)


class Cells:
    def __init__(self, cells_x, count, ys):
        plane = count * count
        self.count = count
        self.parts = [
            [(x, y) for x in range(cells_x) for y in ys if y * plane % lanes == shift] for shift in (0, lanes // 2)
        ]
        self.order = self.parts[0] + self.parts[1]
        self.size = len(self.order) * count

    def rows(self, x, y):
        at = self.order.index((x, y)) * self.count
        return slice(at, at + self.count)

    def part_rows(self, k):
        at = k * len(self.parts[0]) * self.count
        return slice(at, at + len(self.parts[k]) * self.count)


def two_rims(refs):
    return (refs[0].at[0], refs[0].at[1]) if len(refs) == 1 else refs


def first_kernel(
    count, rest, cells, cells_y,
    density_ref, below_ref, above_ref, a_ref, b_ref, loss_ref,
    inverse_ref, forward_ref, rows_ref, speed_ref, moves_ref,
    field_ref, *refs,
):
    up_ref, down_ref = two_rims(refs[:-3])
    modes_ref, sum_ref, rim_ref = refs[-3:]
    cells_x = density_ref.shape[0]
    middle = count // 2
    plane = count * count
    for i in range(2):
        rim_ref[i, :middle] = above_ref[i]
        rim_ref[i, middle:] = below_ref[i]
    positive = lax.broadcasted_iota(jnp.int32, (count, 1), 0) >= middle

    def behind(x):
        return density_ref[x] if x >= 0 else rim_ref[x + 2]

    def ahead(x):
        return density_ref[x] if x < cells_x else rim_ref[x - cells_x]

    w0, w1, w2 = [speed_ref[:, k : k + 1] for k in range(3)]
    moved_on = []
    for x in range(cells_x):
        near = jnp.where(positive, behind(x - 1), ahead(x + 1))
        far = jnp.where(positive, behind(x - 2), ahead(x + 2))
        moved_on.append(w0 * density_ref[x] + w1 * near + w2 * far)
    for k, part in enumerate(cells.parts):
        starts = [(x, y * plane // lanes * lanes) for x, y in part]
        values = jnp.concatenate([moved_on[x][:, at : at + 5 * lanes] for x, at in starts], axis=0)
        field_ref[cells.part_rows(k)] = moved_tiles(values, moves_ref[k])
    collide(field_ref, modes_ref, sum_ref, a_ref, b_ref, loss_ref, inverse_ref, forward_ref, rows_ref, count, rest, 2)
    for x in range(cells_x):
        for k in range(2):
            up_ref[x, k] = field_ref[cells.rows(x, cells_y - 2 + k), 2 * lanes :]
            down_ref[x, k, :, : 2 * lanes] = field_ref[cells.rows(x, k), : 2 * lanes]
            down_ref[x, k, :, 2 * lanes :] = field_ref[cells.rows(x, k), 4 * lanes :]


def sweep_y(given_ref, below_ref, above_ref, speed_ref, field_ref, everything, cells, cells_y, rest):
    backward_last = (lane_index() // (2 * rest)) % 2 == 1

    def cell(x, y, part):
        if y < 0:
            return below_ref[x, y + 2, :, (part - 2) * lanes : (part - 1) * lanes]
        if y >= cells_y:
            at = part if part < 2 else 2
            return above_ref[x, y - cells_y, :, at * lanes : (at + 1) * lanes]
        return given_ref[everything.rows(x, y), part * lanes : (part + 1) * lanes]

    for x, y in cells.order:
        for part in range(5):
            w0, w1, w2 = [speed_ref[k : k + 1, part * lanes : (part + 1) * lanes] for k in range(3)]
            if part < 2:
                near, far = cell(x, y + 1, part), cell(x, y + 2, part)
            elif part < 4:
                near, far = cell(x, y - 1, part), cell(x, y - 2, part)
            else:
                near = jnp.where(backward_last, cell(x, y - 1, part), cell(x, y + 1, part))
                far = jnp.where(backward_last, cell(x, y - 2, part), cell(x, y + 2, part))
            field_ref[cells.rows(x, y), part * lanes : (part + 1) * lanes] = (
                w0 * cell(x, y, part) + w1 * near + w2 * far
            )


def inner_kernel(
    count, rest, everything, cells, cells_y,
    given_ref, a_ref, b_ref, loss_ref, inverse_ref, forward_ref, rows_ref, speed_ref,
    field_ref, modes_ref, sum_ref,
):
    sweep_y(given_ref, None, None, speed_ref, field_ref, everything, cells, cells_y, rest)
    collide(field_ref, modes_ref, sum_ref, a_ref, b_ref, loss_ref, inverse_ref, forward_ref, rows_ref, count, rest, 4)


def outer_kernel(
    count, rest, everything, inner, cells, cells_y,
    given_ref, inner_ref, a_ref, b_ref, loss_ref, inverse_ref, forward_ref, rows_ref, speed_ref, moves_ref, *refs,
):
    below_ref, above_ref = two_rims(refs[:-4])
    out_ref, field_ref, modes_ref, sum_ref = refs[-4:]
    plane = count * count
    sweep_y(given_ref, below_ref, above_ref, speed_ref, field_ref, everything, cells, cells_y, rest)
    collide(field_ref, modes_ref, sum_ref, a_ref, b_ref, loss_ref, inverse_ref, forward_ref, rows_ref, count, rest, 2)
    pieces = {}
    for k in range(2):
        values = [field_ref[cells.part_rows(k)], inner_ref[inner.part_rows(k)]]
        natural = moved_tiles(jnp.concatenate(values, axis=0), moves_ref[2 + k])
        for i, place in enumerate(cells.parts[k] + inner.parts[k]):
            pieces[place] = natural[i * count : (i + 1) * count]
    for x in range(out_ref.shape[0]):
        filled = {}
        for y in range(cells_y):
            first = y * plane // lanes
            for t in range(5):
                value = tile(pieces[x, y], t)
                filled[first + t] = filled[first + t] + value if first + t in filled else value
        for t in range(out_ref.shape[2] // lanes):
            out_ref[x, :, t * lanes : (t + 1) * lanes] = filled[t]


def body(density, gains_a, gains_b, loss_rates):
    cells_x, count, width = density.shape
    terms = gains_a.shape[0]
    middle = count // 2
    plane = count * count
    cells_y = width // plane
    rest = middle * middle - lanes
    everything = Cells(cells_x, count, range(cells_y))
    inner = Cells(cells_x, count, range(2, cells_y - 2))
    outer = Cells(cells_x, count, [*range(2), *range(cells_y - 2, cells_y)])
    points = point_lanes(count)
    moves = np.full((4, 1, 5 * lanes), -1, np.int32)
    for k in range(2):
        shift = k * lanes // 2
        moves[k, 0] = np.where(points >= 0, points + shift, -1)
        for lane in range(4 * lanes + 4 * rest):
            moves[2 + k, 0, points[lane] + shift] = lane
    weights = courant_weights(count)
    lane_speed = np.where(points >= 0, weights[:, points // count], 0.0).astype(np.float32)
    lane_speed = jnp.asarray(lane_speed)
    row_speed = jnp.asarray(weights.T.astype(np.float32))
    group = min(cells_together(c.size // count) for c in (everything, inner, outer))
    tables = [jnp.asarray(t) for t in (inverse_tables(count), forward_tables(count), row_tables(count, group))]

    def params(mib):
        return pltpu.CompilerParams(vmem_limit_bytes=mib << 20)

    def scratch(cells):
        return [pltpu.VMEM((cells.size, k * lanes), f32) for k in (6, 5)]

    def cost(cells):
        return pl.CostEstimate(flops=cells.size << 27, bytes_accessed=4 << 20, transcendentals=0)

    steps = 2 if terms % 2 == 0 else 1
    taken = terms // steps

    def pack(gains, extra, extra_spec, extra_out_spec, extra_shape):
        return pl.pallas_call(
            functools.partial(pack_kernel, count),
            grid=(steps,),
            in_specs=[
                pl.BlockSpec((1, 6 * lanes), lambda i: (0, 0)),
                pl.BlockSpec((taken * plane, count), lambda i: (i, 0)),
                extra_spec,
            ],
            out_specs=[pl.BlockSpec((taken, count, 6 * lanes), lambda i: (i, 0, 0)), extra_out_spec],
            out_shape=(jax.ShapeDtypeStruct((terms, count, 6 * lanes), f32), extra_shape),
            scratch_shapes=[pltpu.VMEM((plane, 6 * lanes), bf16)],
            compiler_params=params(pack_mib),
            cost_estimate=pl.CostEstimate(flops=2 << 30, bytes_accessed=4 << 20, transcendentals=0),
            name="pack",
        )(
            jnp.asarray(mode_lanes(count)[None]),
            pltpu.with_memory_space_constraint(gains.reshape(-1, count), pltpu.HBM),
            extra,
        )

    below = passed_along(density[-2:, middle:], "gx", 1)
    packed_a, packed_loss = pack(
        gains_a,
        pltpu.with_memory_space_constraint(loss_rates.reshape(-1, count), pltpu.HBM),
        pl.BlockSpec((plane, count), lambda i: (0, 0)),
        pl.BlockSpec((count, 6 * lanes), lambda i: (0, 0)),
        jax.ShapeDtypeStruct((count, 6 * lanes), f32),
    )
    leaving, packed_a, packed_loss, gains_b = lax.optimization_barrier(
        (density[:2, :middle], packed_a, packed_loss, gains_b)
    )
    above = passed_along(leaving, "gx", -1)
    packed_b, move_tables = pack(
        gains_b,
        jnp.asarray(moves),
        pl.BlockSpec((4 // steps, 1, 5 * lanes), lambda i: (i, 0, 0)),
        pl.BlockSpec((4 // steps, 5 * lanes, 5 * lanes), lambda i: (i, 0, 0)),
        jax.ShapeDtypeStruct((4, 5 * lanes, 5 * lanes), bf16),
    )
    rim = (cells_x, 2, count, 3 * lanes)
    mirrored = lax.axis_size("gy") == 2
    rim_shapes = [jax.ShapeDtypeStruct((2, *rim), f32)] if mirrored else [jax.ShapeDtypeStruct(rim, f32)] * 2
    field, *rims = pl.pallas_call(
        functools.partial(first_kernel, count, rest, everything, cells_y),
        out_shape=(jax.ShapeDtypeStruct((everything.size, 5 * lanes), f32), *rim_shapes),
        scratch_shapes=scratch(everything) + [pltpu.VMEM((2, count, width), f32)],
        compiler_params=params(first_mib),
        cost_estimate=cost(everything),
        name="first",
    )(density, below, above, packed_a, packed_b, packed_loss, *tables, row_speed, move_tables)
    rims = [passed_along(value, "gy", steps) for value, steps in zip(rims, (1, -1))]
    inner_field = pl.pallas_call(
        functools.partial(inner_kernel, count, rest, everything, inner, cells_y),
        out_shape=jax.ShapeDtypeStruct((inner.size, 5 * lanes), f32),
        scratch_shapes=scratch(inner),
        compiler_params=params(second_mib),
        cost_estimate=cost(inner),
        name="inner",
    )(field, packed_a, packed_b, packed_loss, *tables, lane_speed)
    return pl.pallas_call(
        functools.partial(outer_kernel, count, rest, everything, inner, outer, cells_y),
        out_shape=jax.ShapeDtypeStruct(density.shape, f32),
        scratch_shapes=[pltpu.VMEM((outer.size, 5 * lanes), f32)] + scratch(outer),
        compiler_params=params(second_mib),
        cost_estimate=cost(outer),
        name="outer",
    )(field, inner_field, packed_a, packed_b, packed_loss, *tables, lane_speed, move_tables, *rims)


def solution(mesh):
    in_specs = (P("gx", None, "gy"), P(), P(), P())
    out_specs = P("gx", None, "gy")
    return jax.shard_map(body, mesh=mesh, in_specs=in_specs, out_specs=out_specs, check_vma=False)
```

```python
import functools

import jax
import jax.numpy as jnp
import numpy as np
from jax import lax
from jax.experimental import pallas as pl
from jax.experimental.pallas import tpu as pltpu
from jax.sharding import PartitionSpec as P

courant_max = 1.6
collide_step = 0.2
lanes = 128
pack_mib, first_mib, second_mib = 24, 28, 24
bf16 = jnp.bfloat16
f32 = jnp.float32
dot = functools.partial(jnp.dot, preferred_element_type=f32)


def passed_along(value, axis, steps):
    count = lax.axis_size(axis)
    pairs = [(source, (source + steps) % count) for source in range(count)]
    return lax.ppermute(value, axis, pairs)


def cosine_table(count):
    freq = np.arange(count)[:, None]
    points = np.arange(count)[None, :]
    scale = np.where(freq == 0, np.sqrt(1.0 / count), np.sqrt(2.0 / count))
    return scale * np.cos(np.pi * (2.0 * points + 1.0) * freq / (2.0 * count))


def two_parts(table):
    high = np.asarray(table, np.float32).astype(bf16)
    return high, (table - high.astype(np.float64)).astype(np.float32).astype(bf16)


def courant_weights(count):
    speeds = np.arange(count) - (count - 1) / 2.0
    a = courant_max * np.abs(speeds) / ((count - 1) / 2.0)
    return np.stack([1.0 - 1.5 * a + 0.5 * a * a, 2.0 * a - a * a, 0.5 * (a * a - a)])


def sign(s, q):
    return -1.0 if ((s >> 1) & (q >> 1)) ^ (s & 1 & q) else 1.0


def block_table(count, q):
    c = cosine_table(count)
    half = count // 2
    return np.kron(c[q >> 1 :: 2, :half], c[q & 1 :: 2, :half])


def point_lanes(count):
    half = count // 2
    block = half * half
    rest = block - lanes
    source = np.full(5 * lanes, -1, np.int32)
    for s in range(4):
        for m in range(block):
            j, l = divmod(m, half)
            y = count - 1 - j if s >> 1 else j
            z = count - 1 - l if s & 1 else l
            if m < lanes:
                source[s * lanes + m] = y * count + z
            else:
                for copy in range(2):
                    source[4 * lanes + copy * 4 * rest + s * rest + m - lanes] = y * count + z
    return source


def mode_lanes(count):
    half = count // 2
    block = half * half
    rest = block - lanes
    source = np.full(6 * lanes, -1, np.int32)
    for q in range(4):
        for m in range(block):
            j, l = divmod(m, half)
            place = (2 * j + (q >> 1)) * count + 2 * l + (q & 1)
            if m < lanes:
                source[q * lanes + m] = place
            else:
                for copy in range(3):
                    source[(4 + q // 2) * lanes + copy * 2 * rest + (q % 2) * rest + m - lanes] = place
    return source


def inverse_tables(count):
    rest = (count // 2) ** 2 - lanes
    out = np.zeros((4, 4 * lanes, 2 * lanes), bf16)
    for q in range(4):
        table = block_table(count, q)
        wide = np.zeros((table.shape[0], 2 * lanes))
        wide[:, :lanes] = table[:, :lanes]
        for s in range(4):
            for copy in range(2):
                at = lanes + copy * 4 * rest + s * rest
                wide[:, at : at + rest] = sign(s, q) * table[:, lanes:]
        high, low = two_parts(wide)
        out[q, :lanes] = high[:lanes]
        out[q, lanes : 2 * lanes] = high[:lanes]
        out[q, 2 * lanes : 3 * lanes] = low[:lanes]
        for copy, part in enumerate((high, high, low)):
            at = 3 * lanes + copy * 2 * rest + (q % 2) * rest
            out[q, at : at + rest] = part[lanes:]
    return out


def forward_tables(count):
    rest = (count // 2) ** 2 - lanes
    out = np.zeros((4, 5 * lanes, 2 * lanes), bf16)
    for q in range(4):
        table = block_table(count, q).T
        wide = np.zeros((table.shape[0], 2 * lanes))
        wide[:, :lanes] = table[:, :lanes]
        for copy in range(3):
            at = lanes + copy * 2 * rest + (q % 2) * rest
            wide[:, at : at + rest] = table[:, lanes:]
        high, low = two_parts(wide)
        out[q, :lanes] = high[:lanes]
        out[q, lanes : 2 * lanes] = high[:lanes]
        out[q, 2 * lanes : 3 * lanes] = low[:lanes]
        for s in range(4):
            for at, part in ((3 * lanes, high), (3 * lanes + 4 * rest, high), (4 * lanes, low)):
                at = at + s * rest
                out[q, at : at + rest] = (sign(s, q) * part[lanes:].astype(np.float32)).astype(bf16)
    return out


def cells_together(cells):
    return max(n for n in (1, 2, 4) if cells % n == 0)


def row_tables(count, cells):
    c = cosine_table(count)
    result = []
    for table in (c, c.T):
        coarse, fine = two_parts(np.kron(np.eye(cells), table))
        upper = np.concatenate([coarse, coarse], axis=1)
        lower = np.concatenate([fine, np.zeros_like(fine)], axis=1)
        result.append(np.concatenate([upper, lower], axis=0))
    return np.stack(result)


def split(value):
    high = value.astype(bf16)
    return high, (value - high.astype(f32)).astype(bf16)


def lane_index():
    return lax.broadcasted_iota(jnp.int32, (1, lanes), 1)


def tile(value, at):
    return value[:, at * lanes : (at + 1) * lanes]


def crossed(v0, v1, v2, v3):
    t0, t1, t2, t3 = v0 + v1, v0 - v1, v2 + v3, v2 - v3
    return t0 + t2, t1 + t3, t0 - t2, t1 - t3


def along_rows(values, table, size):
    parts = [split(value) for value in values]
    found = []
    for at in range(0, values[0].shape[0], size):
        pieces = [jnp.concatenate([high[at : at + size], low[at : at + size]], axis=0) for high, low in parts]
        both = dot(table, jnp.concatenate(pieces, axis=1))
        found.append(both[:size] + both[size:])
    return found


def forward(value, table_ref, rest):
    mixed = crossed(*[tile(value, s) for s in range(4)])
    high, low = split(tile(value, 4))
    both = jnp.where(lane_index() < 4 * rest, high.astype(f32), low.astype(f32)).astype(bf16)
    found = []
    for q in range(4):
        q_high, q_low = split(mixed[q])
        found.append(dot(jnp.concatenate([q_high, q_low, q_high, both, high], axis=1), table_ref[q]))
    return jnp.concatenate(
        [tile(v, 0) for v in found] + [tile(found[0], 1) + tile(found[1], 1), tile(found[2], 1) + tile(found[3], 1)],
        axis=1,
    )


def inverse_plane(modes, table_ref, rest):
    low_lanes = (lane_index() >= 2 * rest) & (lane_index() < 4 * rest)
    both = []
    for pair in range(2):
        value = tile(modes, 4 + pair)
        high = value.astype(bf16).astype(f32)
        both.append(jnp.where(low_lanes, value - high, high).astype(bf16))
    found = []
    for q in range(4):
        high, low = split(tile(modes, q))
        found.append(dot(jnp.concatenate([high, low, high, both[q // 2]], axis=1), table_ref[q]))
    main = crossed(*[tile(v, 0) for v in found])
    last = (tile(found[0], 1) + tile(found[1], 1)) + (tile(found[2], 1) + tile(found[3], 1))
    return jnp.concatenate(list(main) + [last], axis=1)


def collide(field_ref, modes_ref, sum_ref, kernel_ref, loss_ref, inverse_ref, forward_ref, rows_ref, count, rest, most):
    rows = field_ref.shape[0]
    cells = rows // count
    terms = kernel_ref.shape[0]
    together = max(n for n in range(1, most + 1) if terms % n == 0)
    main = 4 * lanes
    size = rows_ref.shape[2] // 2

    def scaled(factor):
        modes = modes_ref[...].reshape(cells, count, 6 * lanes)
        return (modes * factor[None]).reshape(rows, 6 * lanes)

    for k, part in enumerate(along_rows([forward(field_ref[...], forward_ref, rest)], rows_ref[0], size)):
        modes_ref[k * size : (k + 1) * size] = part
    plane = inverse_plane(scaled(loss_ref[...]), inverse_ref, rest)
    for k, part in enumerate(along_rows([plane], rows_ref[1], size)):
        at = slice(k * size, (k + 1) * size)
        sum_ref[at] = -field_ref[at] * part

    def term(step, carry):
        factors = [kernel_ref[together * step + k, side] for k in range(together) for side in range(2)]
        plane = inverse_plane(jnp.concatenate([scaled(f) for f in factors], axis=0), inverse_ref, rest)
        pairs = []
        for k in range(together):
            first, second = [plane[(2 * k + side) * rows : (2 * k + side + 1) * rows] for side in range(2)]
            shared = jnp.where(lane_index() < 4 * rest, tile(first, 4), tile(second, 4))
            pairs.append(jnp.concatenate([first[:, :main], second[:, :main], shared], axis=1))
        for k, part in enumerate(along_rows(pairs, rows_ref[1], size)):
            at = slice(k * size, (k + 1) * size)
            total = sum_ref[at, :main]
            last = sum_ref[at, main:]
            for pair in range(together):
                lane = pair * (2 * main + lanes)
                total = total + part[:, lane : lane + main] * part[:, lane + main : lane + 2 * main]
                shared = part[:, lane + 2 * main : lane + 2 * main + lanes]
                last = last + shared * pltpu.roll(shared, 4 * rest, 1)
            sum_ref[at, :main] = total
            sum_ref[at, main:] = last
        return carry

    lax.fori_loop(0, terms // together, term, 0)
    field_ref[...] = field_ref[...] + collide_step * sum_ref[...]


def one_hot(source_row, rows):
    index = lax.broadcasted_iota(jnp.int32, (rows, source_row.shape[1]), 0)
    return jnp.where(index == source_row, 1.0, 0.0).astype(bf16)


def moved(value, table):
    high, low = split(value)
    both = dot(jnp.concatenate([high, low], axis=0), table)
    return both[: value.shape[0]] + both[value.shape[0] :]


def moved_tiles(value, table):
    high, low = split(value)
    return dot(jnp.concatenate([high, low], axis=1), jnp.concatenate([table, table], axis=0))


def pack_kernel(count, source_ref, move_ref, a_ref, b_ref, loss_ref, out_ref, loss_out_ref, moves_ref, table_ref):
    @pl.when(pl.program_id(0) == 0)
    def _():
        table_ref[...] = one_hot(source_ref[...], count * count)

    for k in range(moves_ref.shape[0]):
        moves_ref[k] = one_hot(move_ref[k], 5 * lanes)

    def rows_of(ref):
        rows = ref.shape[0] // count
        return jnp.concatenate([ref[pl.ds(k, rows, stride=count), :] for k in range(count)], axis=1)

    terms = out_ref.shape[0]
    both = jnp.concatenate([rows_of(a_ref), rows_of(b_ref)], axis=0)
    both = moved(both, table_ref[...]).reshape(2, terms, count, 6 * lanes)
    for side in range(2):
        out_ref[:, side] = both[side]

    @pl.when(pl.program_id(0) == 0)
    def _():
        loss_out_ref[...] = moved(rows_of(loss_ref), table_ref[...])


class Cells:
    def __init__(self, cells_x, count, ys):
        plane = count * count
        self.count = count
        self.parts = [
            [(x, y) for x in range(cells_x) for y in ys if y * plane % lanes == shift] for shift in (0, lanes // 2)
        ]
        self.order = self.parts[0] + self.parts[1]
        self.size = len(self.order) * count

    def rows(self, x, y):
        at = self.order.index((x, y)) * self.count
        return slice(at, at + self.count)

    def part_rows(self, k):
        at = k * len(self.parts[0]) * self.count
        return slice(at, at + len(self.parts[k]) * self.count)


def two_rims(refs):
    return (refs[0], refs[0]) if len(refs) == 1 else refs


def backward_lanes(rest):
    return (lane_index() // (2 * rest)) % 2 == 1


def first_kernel(
    count, rest, cells, cells_y,
    density_ref, below_ref, above_ref, kernel_ref, loss_ref, inverse_ref, forward_ref, rows_ref, speed_ref, moves_ref,
    field_ref, *refs,
):
    up_ref, down_ref = two_rims(refs[:-3])
    modes_ref, sum_ref, rim_ref = refs[-3:]
    cells_x = density_ref.shape[0]
    middle = count // 2
    plane = count * count
    for i in range(2):
        rim_ref[i, :middle] = above_ref[i]
        rim_ref[i, middle:] = below_ref[i]
    positive = lax.broadcasted_iota(jnp.int32, (count, 1), 0) >= middle

    def behind(x):
        return density_ref[x] if x >= 0 else rim_ref[x + 2]

    def ahead(x):
        return density_ref[x] if x < cells_x else rim_ref[x - cells_x]

    w0, w1, w2 = [speed_ref[:, k : k + 1] for k in range(3)]
    moved_on = []
    for x in range(cells_x):
        near = jnp.where(positive, behind(x - 1), ahead(x + 1))
        far = jnp.where(positive, behind(x - 2), ahead(x + 2))
        moved_on.append(w0 * density_ref[x] + w1 * near + w2 * far)
    for k, part in enumerate(cells.parts):
        starts = [(x, y * plane // lanes * lanes) for x, y in part]
        values = jnp.concatenate([moved_on[x][:, at : at + 5 * lanes] for x, at in starts], axis=0)
        field_ref[cells.part_rows(k)] = moved_tiles(values, moves_ref[k])
    collide(field_ref, modes_ref, sum_ref, kernel_ref, loss_ref, inverse_ref, forward_ref, rows_ref, count, rest, 2)
    for x in range(cells_x):
        for k in range(2):
            up, down = cells.rows(x, cells_y - 2 + k), cells.rows(x, k)
            down_ref[x, k, :, : 2 * lanes] = field_ref[down, : 2 * lanes]
            if up_ref is down_ref:
                up_ref[x, k, :, 2 * lanes : 4 * lanes] = field_ref[up, 2 * lanes : 4 * lanes]
                up_ref[x, k, :, 4 * lanes :] = jnp.where(
                    backward_lanes(rest), field_ref[up, 4 * lanes :], field_ref[down, 4 * lanes :]
                )
            else:
                up_ref[x, k] = field_ref[up, 2 * lanes :]
                down_ref[x, k, :, 2 * lanes :] = field_ref[down, 4 * lanes :]


def sweep_y(given_ref, below_ref, above_ref, speed_ref, field_ref, everything, cells, cells_y, rest):
    backward_last = backward_lanes(rest)

    def cell(x, y, part):
        if below_ref is above_ref and not 0 <= y < cells_y:
            return below_ref[x, y % cells_y % (cells_y - 2), :, part * lanes : (part + 1) * lanes]
        if y < 0:
            return below_ref[x, y + 2, :, (part - 2) * lanes : (part - 1) * lanes]
        if y >= cells_y:
            at = part if part < 2 else 2
            return above_ref[x, y - cells_y, :, at * lanes : (at + 1) * lanes]
        return given_ref[everything.rows(x, y), part * lanes : (part + 1) * lanes]

    for x, y in cells.order:
        for part in range(5):
            w0, w1, w2 = [speed_ref[k : k + 1, part * lanes : (part + 1) * lanes] for k in range(3)]
            if part < 2:
                near, far = cell(x, y + 1, part), cell(x, y + 2, part)
            elif part < 4:
                near, far = cell(x, y - 1, part), cell(x, y - 2, part)
            else:
                near = jnp.where(backward_last, cell(x, y - 1, part), cell(x, y + 1, part))
                far = jnp.where(backward_last, cell(x, y - 2, part), cell(x, y + 2, part))
            field_ref[cells.rows(x, y), part * lanes : (part + 1) * lanes] = (
                w0 * cell(x, y, part) + w1 * near + w2 * far
            )


def inner_kernel(
    count, rest, everything, cells, cells_y,
    given_ref, kernel_ref, loss_ref, inverse_ref, forward_ref, rows_ref, speed_ref,
    field_ref, modes_ref, sum_ref,
):
    sweep_y(given_ref, None, None, speed_ref, field_ref, everything, cells, cells_y, rest)
    collide(field_ref, modes_ref, sum_ref, kernel_ref, loss_ref, inverse_ref, forward_ref, rows_ref, count, rest, 4)


def outer_kernel(
    count, rest, everything, inner, cells, cells_y,
    given_ref, inner_ref, kernel_ref, loss_ref, inverse_ref, forward_ref, rows_ref, speed_ref, moves_ref, *refs,
):
    below_ref, above_ref = two_rims(refs[:-4])
    out_ref, field_ref, modes_ref, sum_ref = refs[-4:]
    plane = count * count
    sweep_y(given_ref, below_ref, above_ref, speed_ref, field_ref, everything, cells, cells_y, rest)
    collide(field_ref, modes_ref, sum_ref, kernel_ref, loss_ref, inverse_ref, forward_ref, rows_ref, count, rest, 2)
    pieces = {}
    for k in range(2):
        values = [field_ref[cells.part_rows(k)], inner_ref[inner.part_rows(k)]]
        natural = moved_tiles(jnp.concatenate(values, axis=0), moves_ref[2 + k])
        for i, place in enumerate(cells.parts[k] + inner.parts[k]):
            pieces[place] = natural[i * count : (i + 1) * count]
    for x in range(out_ref.shape[0]):
        filled = {}
        for y in range(cells_y):
            first = y * plane // lanes
            for t in range(5):
                value = tile(pieces[x, y], t)
                filled[first + t] = filled[first + t] + value if first + t in filled else value
        for t in range(out_ref.shape[2] // lanes):
            out_ref[x, :, t * lanes : (t + 1) * lanes] = filled[t]


def body(density, gains_a, gains_b, loss_rates):
    cells_x, count, width = density.shape
    terms = gains_a.shape[0]
    middle = count // 2
    plane = count * count
    cells_y = width // plane
    rest = middle * middle - lanes
    everything = Cells(cells_x, count, range(cells_y))
    inner = Cells(cells_x, count, range(2, cells_y - 2))
    outer = Cells(cells_x, count, [*range(2), *range(cells_y - 2, cells_y)])
    points = point_lanes(count)
    moves = np.full((4, 1, 5 * lanes), -1, np.int32)
    for k in range(2):
        shift = k * lanes // 2
        moves[k, 0] = np.where(points >= 0, points + shift, -1)
        for lane in range(4 * lanes + 4 * rest):
            moves[2 + k, 0, points[lane] + shift] = lane
    weights = courant_weights(count)
    lane_speed = np.where(points >= 0, weights[:, points // count], 0.0).astype(np.float32)
    lane_speed = jnp.asarray(lane_speed)
    row_speed = jnp.asarray(weights.T.astype(np.float32))
    group = min(cells_together(c.size // count) for c in (everything, inner, outer))
    tables = [jnp.asarray(t) for t in (inverse_tables(count), forward_tables(count), row_tables(count, group))]

    def params(mib):
        return pltpu.CompilerParams(vmem_limit_bytes=mib << 20)

    def scratch(cells):
        return [pltpu.VMEM((cells.size, k * lanes), f32) for k in (6, 5)]

    def cost(cells):
        return pl.CostEstimate(flops=cells.size << 27, bytes_accessed=4 << 20, transcendentals=0)

    below = passed_along(density[-2:, middle:], "gx", 1)
    above = passed_along(density[:2, :middle], "gx", -1)
    steps = 2 if terms % 2 == 0 else 1
    taken = terms // steps
    gain_spec = pl.BlockSpec((taken * plane, count), lambda i: (i, 0))
    packed, packed_loss, move_tables = pl.pallas_call(
        functools.partial(pack_kernel, count),
        grid=(steps,),
        in_specs=[
            pl.BlockSpec((1, 6 * lanes), lambda i: (0, 0)),
            pl.BlockSpec((4 // steps, 1, 5 * lanes), lambda i: (i, 0, 0)),
            gain_spec,
            gain_spec,
            pl.BlockSpec((plane, count), lambda i: (0, 0)),
        ],
        out_specs=[
            pl.BlockSpec((taken, 2, count, 6 * lanes), lambda i: (i, 0, 0, 0)),
            pl.BlockSpec((count, 6 * lanes), lambda i: (0, 0)),
            pl.BlockSpec((4 // steps, 5 * lanes, 5 * lanes), lambda i: (i, 0, 0)),
        ],
        out_shape=(
            jax.ShapeDtypeStruct((terms, 2, count, 6 * lanes), f32),
            jax.ShapeDtypeStruct((count, 6 * lanes), f32),
            jax.ShapeDtypeStruct((4, 5 * lanes, 5 * lanes), bf16),
        ),
        scratch_shapes=[pltpu.VMEM((plane, 6 * lanes), bf16)],
        compiler_params=params(pack_mib),
        cost_estimate=pl.CostEstimate(flops=4 << 30, bytes_accessed=8 << 20, transcendentals=0),
        name="pack",
    )(
        jnp.asarray(mode_lanes(count)[None]),
        jnp.asarray(moves),
        gains_a.reshape(-1, count),
        gains_b.reshape(-1, count),
        loss_rates.reshape(-1, count),
    )
    rim = (cells_x, 2, count, 3 * lanes)
    mirrored = lax.axis_size("gy") == 2
    rim_shapes = [jax.ShapeDtypeStruct((*rim[:3], 5 * lanes), f32)] if mirrored else [jax.ShapeDtypeStruct(rim, f32)] * 2
    field, *rims = pl.pallas_call(
        functools.partial(first_kernel, count, rest, everything, cells_y),
        out_shape=(jax.ShapeDtypeStruct((everything.size, 5 * lanes), f32), *rim_shapes),
        scratch_shapes=scratch(everything) + [pltpu.VMEM((2, count, width), f32)],
        compiler_params=params(first_mib),
        cost_estimate=cost(everything),
        name="first",
    )(density, below, above, packed, packed_loss, *tables, row_speed, move_tables)
    rims = [passed_along(value, "gy", steps) for value, steps in zip(rims, (1, -1))]
    inner_field = pl.pallas_call(
        functools.partial(inner_kernel, count, rest, everything, inner, cells_y),
        out_shape=jax.ShapeDtypeStruct((inner.size, 5 * lanes), f32),
        scratch_shapes=scratch(inner),
        compiler_params=params(second_mib),
        cost_estimate=cost(inner),
        name="inner",
    )(field, packed, packed_loss, *tables, lane_speed)
    return pl.pallas_call(
        functools.partial(outer_kernel, count, rest, everything, inner, outer, cells_y),
        out_shape=jax.ShapeDtypeStruct(density.shape, f32),
        scratch_shapes=[pltpu.VMEM((outer.size, 5 * lanes), f32)] + scratch(outer),
        compiler_params=params(second_mib),
        cost_estimate=cost(outer),
        name="outer",
    )(field, inner_field, packed, packed_loss, *tables, lane_speed, move_tables, *rims)


def solution(mesh):
    in_specs = (P("gx", None, "gy"), P(), P(), P())
    out_specs = P("gx", None, "gy")
    return jax.shard_map(body, mesh=mesh, in_specs=in_specs, out_specs=out_specs, check_vma=False)
```
